128 devices in a mesh: cls: 4 (over y), rows: 32 (over z, x, core).
Axes of the slice: x: 4, y: 4, z: 4, core: 2. Of those that a mesh axis runs over, the one named last changes fastest.
Arguments:
- prior: bfloat16 [65536, 1000], P('rows', 'cls'), may hold values from -6 to 6
- blocks: bfloat16 [256, 24, 256, 256], P('rows'), may hold values from -0.078125 to 0.078125
- links: int32 [256, 24], P('rows'), may hold values from 0 to 39, as said below
- counts: int32 [256], P('rows'), may hold values from 1 to 24
- fetch: int32 [32, 32, 1], P('rows'), may hold values from 0 to 7
- seeds: int32 [65536], P('rows'), may hold values from -1000 to 999
- inv_temp: float32 [65536], P('rows'), may hold values from 1 to 300
Outputs:
- pseudo: bfloat16 [65536, 1000], P('rows', 'cls')
- certainty: float32 [65536], P('rows')
The draws below stay inside these ranges and needn't reach their ends.
Inputs may be any that keep to these rules, and one draw needn't show every extreme that they name: links index a slot list of 8 own tiles followed by one tile from each index of rows in order; every one of these slots is named by some link of its index of rows. `seeds`: a negative seed marks an image without a label.
All inputs are finite; a program needn't handle non-finite values.
Results may differ from the reference program's by a relative error of at most 0.0075.
The reference program's roundings to bfloat16 on the way (of `first`) count: a program that leaves them out, or rounds other values in their place, can miss the bound.
Values may be sent and summed in bfloat16 or wider, within the bound.
A program may use at most 192 MiB of HBM per device.

```python
import math
import jax
import jax.numpy as jnp
from jax import lax

TILE = 256
CLS = 1000
NB = 24
TPD = 8
CAP = 1
TILES = 256
ROWS = 65536
N_ROWS = 32


def draw_links(key, part):
    slot_total = TPD + N_ROWS * CAP

    def per_device(subkey):
        key_extra, key_order = jax.random.split(subkey)
        extra = jax.random.randint(key_extra, (TPD * NB - slot_total,), 0, slot_total, dtype=jnp.int32)
        position_entries = jnp.concatenate([jnp.arange(slot_total, dtype=jnp.int32), extra])
        return jax.random.permutation(key_order, position_entries)
    return jax.vmap(per_device)(jax.random.split(key, N_ROWS)).reshape(TPD * N_ROWS, NB)


def draw_counts(key, part):
    values = jax.random.randint(key, (TPD * N_ROWS,), 1, NB + 1, dtype=jnp.int32)
    return values.at[0].set(NB).at[1].set(1)


def draw_fetch(key, part):
    scores = jax.random.randint(key, (N_ROWS, N_ROWS, TPD), 0, 1 << 20, dtype=jnp.int32)
    scores = scores * TPD + jnp.arange(TPD, dtype=jnp.int32)
    order = jnp.argsort(scores, axis=-1, stable=True).astype(jnp.int32)
    selected_entries = order[..., :CAP]
    return selected_entries.at[0, 0, 0].set(TPD - 1).at[0, 1, 0].set(0)


def draw_inv_temp(key, part):
    key_base = jax.random.fold_in(key, 0)
    base = jnp.exp(jax.random.uniform(key_base, (ROWS,), jnp.float32, 0.0, math.log(8.0)))
    return base


def place_ends(entries, rng, low, largest):
    spot = [jax.random.randint(jax.random.fold_in(rng, axis), (), 0, length) for axis, length in enumerate(entries.shape)]
    widest = entries.shape.index(max(entries.shape))
    neighbour = spot[:widest] + [(spot[widest] + 1) % entries.shape[widest]] + spot[widest + 1:]
    return entries.at[tuple(spot)].set(low).at[tuple(neighbour)].set(largest)


def level_of(rng, shape, shards, least, high):
    def one(position, shards_of):
        heights = jax.random.uniform(jax.random.fold_in(jax.random.fold_in(rng, 6), position), (shards_of,), jnp.float32, least / len(shards), high / len(shards))
        return jnp.repeat(jnp.exp(heights), shape[position] // shards_of).reshape((-1,) + (1,) * (len(shape) - position - 1))

    factor_of = one(*shards[0])
    for cut in shards[1:]:
        factor_of = factor_of * one(*cut)
    return factor_of


def centred(own_key, dims, width, reach, cuts=(), held_as=jnp.bfloat16):
    level = level_of(own_key, dims, cuts, -0.22, 0.18) if cuts else 1.0
    values = jax.random.normal(own_key, dims, jnp.float32) * width * level
    return jnp.minimum(jnp.maximum(values, -reach), reach).astype(held_as)


def setup_inputs(seed: int = 0) -> dict:
    splits = jax.random.split(jax.random.key(seed), 8)
    return {
        "prior": centred(splits[0], (ROWS, CLS), 1.0, 6.0, ((0, 32), (1, 4))),
        "blocks": centred(splits[1], (TILES, NB, TILE, TILE), (NB * TILE) ** -0.5, 0.078125, ((0, 32),)),
        "links": draw_links(jax.random.fold_in(splits[7], 71), 0),
        "counts": draw_counts(jax.random.fold_in(splits[7], 71), 0),
        "fetch": draw_fetch(jax.random.fold_in(splits[7], 71), 0),
        "seeds": place_ends(jax.random.randint(splits[5], (ROWS,), -CLS, CLS), jax.random.fold_in(splits[5], 1), -CLS, CLS - 1).astype(jnp.int32),
        "inv_temp": draw_inv_temp(jax.random.fold_in(splits[7], 71), 0),
    }


blend = 0.8


def column_block_list(links, fetch):
    owner = (jnp.arange(links.shape[0], dtype=jnp.int32) // TPD)[:, None]
    remote = jnp.maximum(links - TPD, 0)
    source = remote // CAP
    place = remote % CAP
    fetched = fetch[owner, source, place]
    return jnp.where(links < TPD, owner * TPD + links, source * TPD + fetched).astype(jnp.int32)


def propagate(field, blocks, tiles_used, live_slots, targets):
    tiled = field.reshape(TILES, TILE, CLS)

    def one_tile(tile_no):
        adjacent_blocks = tiled[tiles_used[tile_no]].astype(jnp.float32)
        adjacent_blocks = jnp.where(live_slots[tile_no][:, None, None], adjacent_blocks, jnp.float32(0.0))
        return jnp.einsum("jab,jbc->ac", blocks[tile_no].astype(jnp.float32), adjacent_blocks)

    accumulated_sum = lax.map(one_tile, jnp.arange(TILES, dtype=jnp.int32))
    return blend * accumulated_sum.reshape(ROWS, CLS) + (1.0 - blend) * targets


def reference(prior, blocks, links, counts, fetch, seeds, inv_temp):
    tiles_used = column_block_list(links, fetch)
    live_slots = jnp.arange(NB, dtype=jnp.int32)[None, :] < counts[:, None]
    targets = (seeds[:, None] == jnp.arange(CLS, dtype=jnp.int32)[None, :]).astype(jnp.float32)
    first = propagate(prior, blocks, tiles_used, live_slots, targets).astype(jnp.bfloat16)
    second = propagate(first, blocks, tiles_used, live_slots, targets)
    logits = inv_temp[:, None] * second
    top = jnp.max(logits, axis=1, keepdims=True)
    shifted = logits - top
    expo = jnp.exp(shifted)
    totals = jnp.sum(expo, axis=1)
    moments = jnp.sum(expo * shifted, axis=1)
    pseudo = (expo / totals[:, None]).astype(jnp.bfloat16)
    certainty = 1.0 - (jnp.log(totals) - moments / totals) / jnp.log(jnp.float32(CLS))
    return pseudo, certainty
```

```python
import functools
import math

import jax
import jax.numpy as jnp
from jax import lax
from jax.experimental import pallas as pl
from jax.experimental.pallas import tpu as pltpu
from jax.sharding import PartitionSpec as P

CLS = 1000
NB = 24
TPD = 8
TILE = 256
W = 250
HALF = 128
Q = 64
ZERO = 40

BLEND = 0.8
MESH = pl.DeviceIdType.MESH

R1, R2, L1, L2, FR, FL, RR, RL, D0R, D1R, D0L, D1L, WR, WL, PT = range(15)

PEERS = [(0, dz, dc) for dz in range(4) for dc in range(2) if (dz, dc) != (0, 0)] + [
    (dx, 0, dc) for dx in range(1, 4) for dc in range(2)
]


def kernel(
    tab_a, tab_b, fetch_row, prior_hbm, blocks_hbm, seeds_ref, temp_ref,
    pseudo_hbm, cert_ref,
    *scratch,
):
    (pv, bv, acc, fld0, fld1, stage, frv, frm, seed_c, temp_c, stats, outv) = scratch[:12]
    gb = scratch[12:20]
    rl = scratch[20:28]
    cs = scratch[28:36]
    (send, recv, f_send, f_recv, y_send, y_recv, b_sem, loc) = scratch[36:]
    fld = (fld0, fld1)

    r = lax.axis_index("rows")
    y = lax.axis_index("cls")
    c = lax.rem(r, 2)
    x = lax.rem(r // 2, 4)
    z = r // 8

    def dev(dx, dz, dc):
        row = (lax.rem(z + dz, 4) * 4 + lax.rem(x + dx, 4)) * 2 + lax.rem(c + dc, 2)
        return (y, row)

    def idx(rnd, rt, kh):
        return (rnd * 2 + rt) * 2 + kh

    def step(rt, d, dc):
        return dev(0, d % 4, dc) if rt == 0 else dev(d % 4, 0, dc)

    def gstep(rt, d):
        return dev(d % 4, 0, 0) if rt == 0 else dev(0, d % 4, 0)

    prior_cp = pltpu.make_async_copy(prior_hbm, pv, loc.at[0])
    prior_cp.start()
    block_cps = [
        pltpu.make_async_copy(blocks_hbm.at[t], bv.at[t], b_sem.at[t]) for t in range(TPD)
    ]
    barrier = pltpu.get_barrier_semaphore()
    for p in PEERS:
        pl.semaphore_signal(barrier, inc=1, device_id=dev(*p), device_id_type=MESH)
    for dy in range(1, 4):
        pl.semaphore_signal(
            barrier, inc=1, device_id=(lax.rem(y + dy, 4), r), device_id_type=MESH
        )
    frv[0] = fetch_row[...]
    frv[8] = fetch_row[...]
    prior_cp.wait()
    for t in range(TPD):
        fld0[t, :, HALF:] = jnp.zeros((TILE, HALF), jnp.bfloat16)
        fld0[t, :, :W] = pv[t * TILE : (t + 1) * TILE, :]
    pl.semaphore_wait(barrier, len(PEERS) + 3)

    def g_copy(rnd, rt, kh, name):
        i = idx(rnd, rt, kh)
        lo, hi = slice(0, 4), slice(4, 8)
        rows = pl.ds(kh * HALF + rt * Q, Q)
        own = fld[rnd]
        src, dst, d = {
            R1: (own.at[lo, rows, :], gb[i].at[2, lo], 1),
            R2: (own.at[hi, rows, :], gb[i].at[2, hi], 1),
            L1: (own.at[hi, rows, :], gb[i].at[0, hi], -1),
            L2: (own.at[lo, rows, :], gb[i].at[0, lo], -1),
            FR: (gb[i].at[2, lo], gb[i].at[1, lo], 1),
            FL: (gb[i].at[0, hi], gb[i].at[1, hi], -1),
        }[name]
        return pltpu.make_async_remote_copy(
            src_ref=src, dst_ref=dst, send_sem=send.at[idx(0, rt, kh), name],
            recv_sem=recv.at[i, name], device_id=gstep(rt, d), device_id_type=MESH,
        )

    def p_copy(rnd, rt, kh, name):
        i = idx(rnd, rt, kh)
        s = idx(0, rt, kh)
        group = lambda g: stage.at[s, g]
        slot = lambda d, dc: cs[i].at[pl.ds((d * 2 + dc) * 4, 4)]
        src, dst, d, dc = {
            RR: (group(2), rl[i].at[0], 1, 0),
            RL: (group(3), rl[i].at[1], -1, 0),
            D0R: (group(0), slot(3, 0), 1, 0),
            D1R: (group(1), slot(3, 1), 1, 1),
            D0L: (group(4), slot(1, 0), -1, 0),
            D1L: (group(5), slot(1, 1), -1, 1),
            WR: (rl[i].at[0], slot(2, 0), 1, 0),
            WL: (rl[i].at[1], slot(2, 1), -1, 1),
            PT: (group(6), slot(0, 1), 0, 1),
        }[name]
        return pltpu.make_async_remote_copy(
            src_ref=src, dst_ref=dst, send_sem=send.at[s, name],
            recv_sem=recv.at[i, name], device_id=step(rt, d, dc), device_id_type=MESH,
        )

    def start_g(rnd, kh, names):
        for name in names:
            for rt in range(2):
                g_copy(rnd, rt, kh, name).start()

    def wait_g(rnd, kh, names):
        for name in names:
            for rt in range(2):
                g_copy(rnd, rt, kh, name).wait_recv()

    def start_p(rnd, kh, names):
        for name in names:
            for rt in range(2):
                p_copy(rnd, rt, kh, name).start()

    def wait_p(rnd, kh, names):
        for name in names:
            for rt in range(2):
                p_copy(rnd, rt, kh, name).wait_recv()

    def wait_sends(kh, rnd):
        for rt in range(2):
            for name in (R1, R2, L1, L2, FR, FL):
                g_copy(rnd, rt, kh, name).wait_send()
            for name in (RR, RL, D0R, D1R, D0L, D1L, WR, WL, PT):
                p_copy(rnd, rt, kh, name).wait_send()

    f_copies = []
    for k, (dx, dz, dc, base) in enumerate(
        [(0, dz, dc, 0) for dz in range(4) for dc in range(2) if (dz, dc) != (0, 0)]
        + [(dx, 0, dc, 8) for dx in range(4) for dc in range(2) if (dx, dc) != (0, 0)]
    ):
        d = dz if base == 0 else dx
        f_copies.append(
            pltpu.make_async_remote_copy(
                src_ref=fetch_row, dst_ref=frv.at[base + ((4 - d) % 4) * 2 + dc],
                send_sem=f_send.at[k], recv_sem=f_recv.at[k],
                device_id=dev(dx, dz, dc), device_id_type=MESH,
            )
        )

    def src_row(rt, d):
        if rt == 0:
            return (z * 4 + lax.rem(x + d, 4)) * 2 + c
        return (lax.rem(z + d, 4) * 4 + x) * 2 + c

    def select(rnd, kh):
        for rt in range(2):
            i = idx(rnd, rt, kh)
            rows = pl.ds(kh * HALF + rt * Q, Q)
            for d in range(4):
                row = src_row(rt, d)
                for dd in (2, 1, 3, 0):
                    for dc in range(2):
                        f = frm[rt * 8 + dd * 2 + dc, 0, row]
                        value = fld[rnd][f, rows, :] if d == 0 else gb[i][d - 1, f]
                        if (dd, dc) == (0, 0):
                            cs[i][d] = value
                        else:
                            g = 6 if dd == 0 else (dd - 1) * 2 + dc
                            stage[idx(0, rt, kh), g, d] = value

    def own_slots(rnd, t):
        for rt in range(2):
            for kh in range(2):
                a = kh * HALF + rt * Q
                cs[idx(rnd, rt, kh)][4 * TPD + t] = fld[rnd][t, a : a + Q, :]

    def product(rnd, kh, t):
        a = idx(rnd, 0, kh)
        b = idx(rnd, 1, kh)
        total = None
        for jp in range(NB // 2):
            left, right = [], []
            for j in (2 * jp, 2 * jp + 1):
                left.append(bv[t, j, :, kh * HALF : (kh + 1) * HALF])
                right.append(cs[a][tab_a[t * NB + j]])
                right.append(cs[b][tab_b[t * NB + j]])
            d = jnp.dot(
                jnp.concatenate(left, axis=1), jnp.concatenate(right, axis=0),
                preferred_element_type=jnp.float32,
            )
            total = d if total is None else total + d
        return total

    lane = lax.broadcasted_iota(jnp.int32, (TILE, TILE), 1)
    inside = lane < W
    column = lane + y * W

    def mixed(t, total):
        hit = (seed_c[t] == column) & inside
        return BLEND * total + jnp.where(hit, jnp.float32(1.0 - BLEND), jnp.float32(0.0))

    HOP1 = (R1, L1)
    HOP1B = (R2, L2)
    FWD = (FR, FL)
    SENDS = (RR, RL, D0R, D0L, D1R, D1L, PT)
    RELAY = (WR, WL)
    FINAL = (D0R, D0L, D1R, D1L, PT, WR, WL)

    start_g(0, 0, HOP1)
    for cp in f_copies:
        cp.start()
    start_g(0, 0, HOP1B)
    for cp in block_cps:
        cp.start()

    for rnd in range(2):
        for rt in range(2):
            for kh in range(2):
                cs[idx(rnd, rt, kh)][ZERO] = jnp.zeros((Q, TILE), jnp.bfloat16)
    for t in range(TPD):
        own_slots(0, t)
    seeds_t = jnp.transpose(seeds_ref[...].astype(jnp.float32), (1, 0))
    temps_t = jnp.transpose(temp_ref[...], (1, 0))
    for t in range(TPD):
        for h in range(2):
            k = 2 * t + h
            seed_c[t, h * HALF : (h + 1) * HALF, :] = seeds_t[:, k : k + 1].astype(jnp.int32)
            temp_c[t, h * HALF : (h + 1) * HALF, :] = temps_t[:, k : k + 1]
    for cp in f_copies:
        cp.wait()
    to_smem = pltpu.make_async_copy(frv, frm, loc.at[1])
    to_smem.start()
    to_smem.wait()

    def exchange(rnd):
        wait_g(rnd, 0, HOP1)
        start_g(rnd, 0, FWD)
        start_g(rnd, 1, HOP1 + HOP1B)
        wait_g(rnd, 0, HOP1B + FWD)
        select(rnd, 0)
        start_p(rnd, 0, SENDS)
        wait_g(rnd, 1, HOP1)
        start_g(rnd, 1, FWD)
        wait_p(rnd, 0, (RR, RL))
        start_p(rnd, 0, RELAY)
        wait_g(rnd, 1, HOP1B + FWD)
        select(rnd, 1)
        start_p(rnd, 1, SENDS)
        wait_p(rnd, 0, FINAL)

    def first_chunk(rnd):
        def body(t, carry):
            @pl.when(t == 4)
            def _():
                wait_p(rnd, 1, (RR, RL))
                start_p(rnd, 1, RELAY)

            acc[t] = product(rnd, 0, t)
            return carry

        lax.fori_loop(0, TPD, body, 0)
        wait_p(rnd, 1, FINAL)

    exchange(0)
    for cp in block_cps:
        cp.wait()
    first_chunk(0)
    for kh in range(2):
        wait_sends(kh, 0)

    def first_tile(t, carry):
        value = mixed(t, acc[t] + product(0, 1, t)).astype(jnp.bfloat16)
        fld1[t] = value
        for rt in range(2):
            for kh in range(2):
                a = kh * HALF + rt * Q
                cs[idx(1, rt, kh)][4 * TPD + t] = value[a : a + Q, :]

        @pl.when(t == 3)
        def _():
            start_g(1, 0, (R1, L2))

        return carry

    lax.fori_loop(0, TPD, first_tile, 0)
    start_g(1, 0, (L1, R2))

    exchange(1)
    first_chunk(1)

    lane128 = lax.broadcasted_iota(jnp.int32, (TILE, HALF), 1)

    def last_tile(t, carry):
        logits = temp_c[t] * mixed(t, acc[t] + product(1, 1, t))
        top = jnp.max(jnp.where(inside, logits, -jnp.inf), axis=1, keepdims=True)
        shifted = jnp.where(inside, logits - top, 0.0)
        expo = jnp.where(inside, jnp.exp(shifted), 0.0)
        acc[t] = expo
        total = jnp.sum(expo, axis=1, keepdims=True)
        moment = jnp.sum(expo * shifted, axis=1, keepdims=True)
        packed = jnp.where(lane128 == 0, top, jnp.where(lane128 == 1, total, moment))
        stats[y, t] = jnp.transpose(packed, (1, 0))[:8, :]
        return carry

    lax.fori_loop(0, TPD, last_tile, 0)

    y_copies = []
    for dy in range(1, 4):
        y_copies.append(
            pltpu.make_async_remote_copy(
                src_ref=stats.at[y], dst_ref=stats.at[y],
                send_sem=y_send.at[dy - 1], recv_sem=y_recv.at[dy - 1],
                device_id=(lax.rem(y + dy, 4), r), device_id_type=MESH,
            )
        )
    for cp in y_copies:
        cp.start()
    for kh in range(2):
        wait_sends(kh, 1)
    for dy in range(1, 4):
        pltpu.make_async_remote_copy(
            src_ref=stats.at[y], dst_ref=stats.at[lax.rem(y + 4 - dy, 4)],
            send_sem=y_send.at[dy - 1], recv_sem=y_recv.at[dy - 1],
            device_id=(lax.rem(y + dy, 4), r), device_id_type=MESH,
        ).wait_recv()
    for cp in y_copies:
        cp.wait_send()

    out_cps = []
    for t in range(TPD):
        parts = [stats[k, t] for k in range(4)]
        tops = [p[0:1, :] for p in parts]
        top = functools.reduce(jnp.maximum, tops)
        total = jnp.zeros((1, TILE), jnp.float32)
        moment = jnp.zeros((1, TILE), jnp.float32)
        for p in parts:
            diff = p[0:1, :] - top
            scale = jnp.exp(diff)
            total = total + scale * p[1:2, :]
            moment = moment + scale * (p[2:3, :] + p[1:2, :] * diff)
        cert = 1.0 - (jnp.log(total) - moment / total) / jnp.log(jnp.float32(CLS))
        cert_ref[2 * t : 2 * t + 1, :] = cert[:, :HALF]
        cert_ref[2 * t + 1 : 2 * t + 2, :] = cert[:, HALF:]
        factor = jnp.exp(stats[y, t][0:1, :] - top) / total
        col = jnp.transpose(jnp.broadcast_to(factor, (8, TILE)), (1, 0))[:, 0:1]
        outv[t * TILE : (t + 1) * TILE, :] = (acc[t] * col).astype(jnp.bfloat16)[:, :W]
        cp = pltpu.make_async_copy(
            outv.at[pl.ds(t * TILE, TILE)], pseudo_hbm.at[pl.ds(t * TILE, TILE)], loc.at[2 + t]
        )
        cp.start()
        out_cps.append(cp)
    for cp in out_cps:
        cp.wait()


def local(prior, blocks, links, counts, fetch, seeds, inv_temp):
    r = lax.axis_index("rows")
    c, x, z = r % 2, (r // 2) % 4, r // 8
    s = jnp.maximum(links - TPD, 0)
    dz = (s // 8 - z) & 3
    dx = ((s // 2) % 4 - x) & 3
    dc = (s - c) & 1
    live = jnp.arange(NB, dtype=jnp.int32)[None, :] < counts[:, None]
    own = links < TPD

    def table(first, second):
        slot = jnp.where(own, 4 * TPD + links, (first * 2 + dc) * 4 + second)
        return jnp.where(live, slot, ZERO).reshape(-1)

    tab_a = table(dz, dx)
    tab_b = table(dx, dz)
    fetch_row = jnp.broadcast_to(jnp.pad(fetch.reshape(1, -1), ((0, 0), (0, 96))), (8, 128))
    bf, f32 = jnp.bfloat16, jnp.float32
    vmem = pltpu.VMEM
    pseudo, cert = pl.pallas_call(
        kernel,
        out_shape=(
            jax.ShapeDtypeStruct((TPD * TILE, W), bf),
            jax.ShapeDtypeStruct((16, 128), f32),
        ),
        in_specs=[
            pl.BlockSpec(memory_space=pltpu.SMEM),
            pl.BlockSpec(memory_space=pltpu.SMEM),
            pl.BlockSpec(memory_space=pltpu.VMEM),
            pl.BlockSpec(memory_space=pl.ANY),
            pl.BlockSpec(memory_space=pl.ANY),
            pl.BlockSpec(memory_space=pltpu.VMEM),
            pl.BlockSpec(memory_space=pltpu.VMEM),
        ],
        out_specs=(pl.BlockSpec(memory_space=pl.ANY), pl.BlockSpec(memory_space=pltpu.VMEM)),
        scratch_shapes=[
            vmem((TPD * TILE, W), bf),
            vmem((TPD, NB, TILE, TILE), bf),
            vmem((TPD, TILE, TILE), f32),
            vmem((TPD, TILE, TILE), bf),
            vmem((TPD, TILE, TILE), bf),
            vmem((4, 7, 4, Q, TILE), bf),
            vmem((16, 8, 128), jnp.int32),
            pltpu.SMEM((16, 8, 128), jnp.int32),
            vmem((TPD, TILE, 1), jnp.int32),
            vmem((TPD, TILE, 1), f32),
            vmem((4, TPD, 8, TILE), f32),
            vmem((TPD * TILE, W), bf),
        ]
        + [vmem((3, TPD, Q, TILE), bf) for _ in range(8)]
        + [vmem((2, 4, Q, TILE), bf) for _ in range(8)]
        + [vmem((ZERO + 1, Q, TILE), bf) for _ in range(8)]
        + [
            pltpu.SemaphoreType.DMA((4, 15)),
            pltpu.SemaphoreType.DMA((8, 15)),
            pltpu.SemaphoreType.DMA((14,)),
            pltpu.SemaphoreType.DMA((14,)),
            pltpu.SemaphoreType.DMA((3,)),
            pltpu.SemaphoreType.DMA((3,)),
            pltpu.SemaphoreType.DMA((TPD,)),
            pltpu.SemaphoreType.DMA((10,)),
        ],
        compiler_params=pltpu.CompilerParams(
            collective_id=0, has_side_effects=True, vmem_limit_bytes=66_000_000
        ),
        name="propagate",
    )(
        tab_a, tab_b, fetch_row, prior, blocks,
        seeds.reshape(16, 128), inv_temp.reshape(16, 128),
    )
    return pseudo, cert.reshape(-1)


def solution(mesh):
    return jax.shard_map(
        local,
        mesh=mesh,
        in_specs=(
            P("rows", "cls"),
            P("rows", None, None, None),
            P("rows", None),
            P("rows"),
            P("rows", None, None),
            P("rows"),
            P("rows"),
        ),
        out_specs=(P("rows", "cls"), P("rows")),
        check_vma=False,
    )
```

```python
import functools
import math

import jax
import jax.numpy as jnp
from jax import lax
from jax.experimental import pallas as pl
from jax.experimental.pallas import tpu as pltpu
from jax.sharding import PartitionSpec as P

CLS = 1000
NB = 24
TPD = 8
TILE = 256
W = 250
HALF = 128
Q = 64
ZERO = 40

BLEND = 0.8
MESH = pl.DeviceIdType.MESH

GR, GL, FR, FL = (0, 1, 2, 3), (4, 5, 6, 7), (8, 9), (10, 11)
RR, RL, D0R, D1R, D0L, D1L, WR, WL, PT = range(12, 21)
NAMES = 21

PEERS = [(0, dz, dc) for dz in range(4) for dc in range(2) if (dz, dc) != (0, 0)] + [
    (dx, 0, dc) for dx in range(1, 4) for dc in range(2)
]


def kernel(
    links_ref, counts_ref, fetch_ref, prior_hbm, blocks_hbm, seeds_ref, temp_ref,
    expo_hbm, stats_out,
    *scratch,
):
    (pv, bv, acc, raw, fld0, fld1, stage, frv, frm, tab_a, tab_b, seed_c, temp_c) = scratch[:13]
    expos, stats = scratch[13:15]
    gb = scratch[15:23]
    rl = scratch[23:31]
    cs = scratch[31:39]
    (send, recv, f_send, f_recv, y_send, y_recv, b_sem, loc) = scratch[39:]
    fld = (fld0, fld1)

    r = lax.axis_index("rows")
    y = lax.axis_index("cls")
    c = lax.rem(r, 2)
    x = lax.rem(r // 2, 4)
    z = r // 8

    def dev(dx, dz, dc):
        row = (lax.rem(z + dz, 4) * 4 + lax.rem(x + dx, 4)) * 2 + lax.rem(c + dc, 2)
        return (y, row)

    def idx(rnd, rt, kh):
        return (rnd * 2 + rt) * 2 + kh

    def step(rt, d, dc):
        return dev(0, d % 4, dc) if rt == 0 else dev(d % 4, 0, dc)

    def gstep(rt, d):
        return dev(d % 4, 0, 0) if rt == 0 else dev(0, d % 4, 0)

    prior_cp = pltpu.make_async_copy(prior_hbm, pv, loc.at[0])
    prior_cp.start()
    block_cps = [
        pltpu.make_async_copy(blocks_hbm.at[t], bv.at[t], b_sem.at[t]) for t in range(TPD)
    ]
    barrier = pltpu.get_barrier_semaphore()
    for p in PEERS:
        pl.semaphore_signal(barrier, inc=1, device_id=dev(*p), device_id_type=MESH)
    for dy in range(1, 4):
        pl.semaphore_signal(
            barrier, inc=1, device_id=(lax.rem(y + dy, 4), r), device_id_type=MESH
        )
    frv[0] = jnp.zeros((8, 128), jnp.int32)
    frv[0, 0:1, 0:32] = fetch_ref[...]
    frv[8] = jnp.zeros((8, 128), jnp.int32)
    frv[8, 0:1, 0:32] = fetch_ref[...]
    prior_cp.wait()
    for t in range(TPD):
        fld0[t, :, HALF:] = jnp.zeros((TILE, HALF), jnp.bfloat16)
        fld0[t, :, :W] = pv[t * TILE : (t + 1) * TILE, :]
    pl.semaphore_wait(barrier, len(PEERS) + 3)

    def g_copy(rnd, rt, kh, name):
        i = idx(rnd, rt, kh)
        rows = pl.ds(kh * HALF + rt * Q, Q)
        if name in GR or name in GL:
            pair = pl.ds(2 * (name % 4), 2)
            d, far = (1, 2) if name in GR else (-1, 0)
            src, dst = fld[rnd].at[pair, rows, :], gb[i].at[far, pair]
        else:
            d, far = (1, 2) if name in FR else (-1, 0)
            pair = pl.ds(2 * (name - 8), 2)
            src, dst = gb[i].at[far, pair], gb[i].at[1, pair]
        return pltpu.make_async_remote_copy(
            src_ref=src, dst_ref=dst, send_sem=send.at[idx(0, rt, kh), name],
            recv_sem=recv.at[i, name], device_id=gstep(rt, d), device_id_type=MESH,
        )

    def p_copy(rnd, rt, kh, name):
        i = idx(rnd, rt, kh)
        s = idx(0, rt, kh)
        group = lambda g: stage.at[s, g]
        slot = lambda d, dc: cs[i].at[pl.ds((d * 2 + dc) * 4, 4)]
        src, dst, d, dc = {
            RR: (group(2), rl[i].at[0], 1, 0),
            RL: (group(3), rl[i].at[1], -1, 0),
            D0R: (group(0), slot(3, 0), 1, 0),
            D1R: (group(1), slot(3, 1), 1, 1),
            D0L: (group(4), slot(1, 0), -1, 0),
            D1L: (group(5), slot(1, 1), -1, 1),
            WR: (rl[i].at[0], slot(2, 0), 1, 0),
            WL: (rl[i].at[1], slot(2, 1), -1, 1),
            PT: (group(6), slot(0, 1), 0, 1),
        }[name]
        return pltpu.make_async_remote_copy(
            src_ref=src, dst_ref=dst, send_sem=send.at[s, name],
            recv_sem=recv.at[i, name], device_id=step(rt, d, dc), device_id_type=MESH,
        )

    def start_g(rnd, kh, names):
        for name in names:
            for rt in range(2):
                g_copy(rnd, rt, kh, name).start()

    def wait_g(rnd, kh, names):
        for name in names:
            for rt in range(2):
                g_copy(rnd, rt, kh, name).wait_recv()

    def start_p(rnd, kh, names):
        for name in names:
            for rt in range(2):
                p_copy(rnd, rt, kh, name).start()

    def wait_p(rnd, kh, names):
        for name in names:
            for rt in range(2):
                p_copy(rnd, rt, kh, name).wait_recv()

    def wait_sends(kh, rnd):
        for rt in range(2):
            for name in GR + GL + FR + FL:
                g_copy(rnd, rt, kh, name).wait_send()
            for name in (RR, RL, D0R, D1R, D0L, D1L, WR, WL, PT):
                p_copy(rnd, rt, kh, name).wait_send()

    f_copies = []
    for k, (dx, dz, dc, base) in enumerate(
        [(0, dz, dc, 0) for dz in range(4) for dc in range(2) if (dz, dc) != (0, 0)]
        + [(dx, 0, dc, 8) for dx in range(4) for dc in range(2) if (dx, dc) != (0, 0)]
    ):
        d = dz if base == 0 else dx
        f_copies.append(
            pltpu.make_async_remote_copy(
                src_ref=frv.at[0], dst_ref=frv.at[base + ((4 - d) % 4) * 2 + dc],
                send_sem=f_send.at[k], recv_sem=f_recv.at[k],
                device_id=dev(dx, dz, dc), device_id_type=MESH,
            )
        )

    def src_row(rt, d):
        if rt == 0:
            return (z * 4 + lax.rem(x + d, 4)) * 2 + c
        return (lax.rem(z + d, 4) * 4 + x) * 2 + c

    def select(rnd, kh):
        for rt in range(2):
            i = idx(rnd, rt, kh)
            rows = pl.ds(kh * HALF + rt * Q, Q)
            for d in range(4):
                row = src_row(rt, d)
                for dd in (2, 1, 3, 0):
                    for dc in range(2):
                        f = frm[rt * 8 + dd * 2 + dc, 0, row]
                        value = fld[rnd][f, rows, :] if d == 0 else gb[i][d - 1, f]
                        if (dd, dc) == (0, 0):
                            cs[i][d] = value
                        else:
                            g = 6 if dd == 0 else (dd - 1) * 2 + dc
                            stage[idx(0, rt, kh), g, d] = value

    def own_slots(rnd, t):
        for rt in range(2):
            for kh in range(2):
                a = kh * HALF + rt * Q
                cs[idx(rnd, rt, kh)][4 * TPD + t] = fld[rnd][t, a : a + Q, :]

    def product(rnd, kh, t):
        a = idx(rnd, 0, kh)
        b = idx(rnd, 1, kh)
        total = None
        for jp in range(NB // 2):
            left, right = [], []
            for j in (2 * jp, 2 * jp + 1):
                left.append(bv[t, j, :, kh * HALF : (kh + 1) * HALF])
                right.append(cs[a][tab_a[t * NB + j]])
                right.append(cs[b][tab_b[t * NB + j]])
            d = jnp.dot(
                jnp.concatenate(left, axis=1), jnp.concatenate(right, axis=0),
                preferred_element_type=jnp.float32,
            )
            total = d if total is None else total + d
        return total

    lane = lax.broadcasted_iota(jnp.int32, (TILE, TILE), 1)
    inside = lane < W
    column = lane + y * W

    def mixed(t, total):
        hit = (seed_c[t] == column) & inside
        return BLEND * total + jnp.where(hit, jnp.float32(1.0 - BLEND), jnp.float32(0.0))

    HOP = ((GR[0], GL[0]), (GR[2], GL[2]), (GR[1], GL[1]), (GR[3], GL[3]))
    ALL_HOPS = sum(HOP, ())
    GO_ON = (((GR[0], FR[0]), (GL[2], FL[0])), ((GR[1], FR[1]), (GL[3], FL[1])))
    REST = (GR[2], GR[3], GL[0], GL[1]) + FR + FL
    SENDS = (RR, RL, D0R, D0L, D1R, D1L, PT)
    RELAY = (WR, WL)
    FINAL = (D0R, D0L, D1R, D1L, PT, WR, WL)

    for cp in f_copies:
        cp.start()
    start_g(0, 0, ALL_HOPS)
    for cp in block_cps:
        cp.start()

    for rnd in range(2):
        for rt in range(2):
            for kh in range(2):
                cs[idx(rnd, rt, kh)][ZERO] = jnp.zeros((Q, TILE), jnp.bfloat16)
    for t in range(TPD):
        own_slots(0, t)

    def forward(rnd, kh):
        for part in GO_ON:
            for name, onward in part:
                wait_g(rnd, kh, (name,))
                start_g(rnd, kh, (onward,))

    def prepare():
        seeds_t = jnp.transpose(seeds_ref[...].astype(jnp.float32), (1, 0))
        temps_t = jnp.transpose(temp_ref[...], (1, 0))
        for t in range(TPD):
            for h in range(2):
                k = 2 * t + h
                seed_c[t, h * HALF : (h + 1) * HALF, :] = seeds_t[:, k : k + 1].astype(jnp.int32)
                temp_c[t, h * HALF : (h + 1) * HALF, :] = temps_t[:, k : k + 1]
        for cp in f_copies:
            cp.wait()
        to_smem = pltpu.make_async_copy(frv, frm, loc.at[1])
        to_smem.start()

        def slots(t, carry):
            count = counts_ref[t]
            for j in range(NB):
                v = links_ref[t, j]
                s = jnp.maximum(v - TPD, 0)
                dz = ((s >> 3) + 4 - z) & 3
                dx = (((s >> 1) & 3) + 4 - x) & 3
                dc = (s + c) & 1
                own = v < TPD
                live = j < count
                sa = jnp.where(own, 4 * TPD + v, (dz * 2 + dc) * 4 + dx)
                sb = jnp.where(own, 4 * TPD + v, (dx * 2 + dc) * 4 + dz)
                tab_a[t * NB + j] = jnp.where(live, sa, ZERO)
                tab_b[t * NB + j] = jnp.where(live, sb, ZERO)
            return carry

        lax.fori_loop(0, TPD, slots, 0)
        to_smem.wait()

    def exchange(rnd):
        forward(rnd, 0)
        start_g(rnd, 1, ALL_HOPS)
        if rnd == 0:
            prepare()
        wait_g(rnd, 0, REST)
        select(rnd, 0)
        forward(rnd, 1)
        start_p(rnd, 0, SENDS)
        wait_g(rnd, 1, REST)
        select(rnd, 1)
        wait_p(rnd, 0, (RR, RL))
        start_p(rnd, 0, RELAY)
        start_p(rnd, 1, SENDS)
        wait_p(rnd, 0, FINAL)

    def first_chunk(rnd):
        def body(t, carry):
            @pl.when(t == 4)
            def _():
                wait_p(rnd, 1, (RR, RL))
                start_p(rnd, 1, RELAY)

            acc[t] = product(rnd, 0, t)
            return carry

        lax.fori_loop(0, TPD, body, 0)
        wait_p(rnd, 1, FINAL)

    exchange(0)
    for cp in block_cps:
        cp.wait()
    first_chunk(0)
    for kh in range(2):
        wait_sends(kh, 0)

    def first_tile(i, carry):
        for k in range(3):

            @pl.when(i == 2 * k + 2)
            def _():
                start_g(1, 0, HOP[k])

        t = (i // 4) * 2 + ((i // 2) % 2) * 4 + i % 2
        value = mixed(t, acc[t] + product(0, 1, t)).astype(jnp.bfloat16)
        fld1[t] = value
        for rt in range(2):
            for kh in range(2):
                a = kh * HALF + rt * Q
                cs[idx(1, rt, kh)][4 * TPD + t] = value[a : a + Q, :]
        return carry

    lax.fori_loop(0, TPD, first_tile, 0)
    start_g(1, 0, HOP[3])

    exchange(1)
    first_chunk(1)

    lane128 = lax.broadcasted_iota(jnp.int32, (TILE, HALF), 1)

    def softmax(t):
        logits = temp_c[t] * mixed(t, raw[...])
        top = jnp.max(jnp.where(inside, logits, -jnp.inf), axis=1, keepdims=True)
        shifted = jnp.where(inside, logits - top, 0.0)
        expo = jnp.where(inside, jnp.exp(shifted), 0.0)
        total = jnp.sum(expo, axis=1, keepdims=True)
        moment = jnp.sum(expo * shifted, axis=1, keepdims=True)
        packed = jnp.where(lane128 == 0, top, jnp.where(lane128 == 1, total, moment))
        return expo, jnp.transpose(packed, (1, 0))[:8, :]

    def keep(t, expo, stat):
        expos[t] = expo
        stats[y, t] = stat

    def y_copy(dy, half, slot):
        tiles = pl.ds(4 * half, 4)
        k = 2 * (dy - 1) + half
        return pltpu.make_async_remote_copy(
            src_ref=stats.at[y, tiles], dst_ref=stats.at[slot, tiles],
            send_sem=y_send.at[k], recv_sem=y_recv.at[k],
            device_id=(lax.rem(y + dy, 4), r), device_id_type=MESH,
        )

    def out_copy(t):
        return pltpu.make_async_copy(expos.at[t], expo_hbm.at[t], loc.at[2 + t])

    def last_tile(t, carry):
        before = jnp.maximum(t - 1, 0)
        expo, stat = softmax(before)
        total = acc[t] + product(1, 1, t)
        keep(before, expo, stat)
        raw[...] = total

        @pl.when(t == 5)
        def _():
            for dy in (2, 1, 3):
                y_copy(dy, 0, y).start()
            for k in range(4):
                out_copy(k).start()

        return carry

    raw[...] = jnp.zeros((TILE, TILE), jnp.float32)
    lax.fori_loop(0, TPD, last_tile, 0)
    keep(TPD - 1, *softmax(TPD - 1))
    for dy in (2, 1, 3):
        y_copy(dy, 1, y).start()
    for k in range(4, TPD):
        out_copy(k).start()
    for kh in range(2):
        wait_sends(kh, 1)
    for k in range(TPD):
        out_copy(k).wait()
    for half in range(2):
        for dy in range(1, 4):
            y_copy(dy, half, y).wait_send()
            y_copy(dy, half, lax.rem(y + 4 - dy, 4)).wait_recv()
    stats_out[...] = stats[...]


def finish(expo_hbm, stats, pseudo_hbm, cert_ref, ev, outv, sem_in, sem_out):
    y = lax.axis_index("cls")
    copies_in, copies_out = [], []
    for t in range(TPD):
        cp = pltpu.make_async_copy(expo_hbm.at[t], ev.at[t], sem_in.at[t])
        cp.start()
        copies_in.append(cp)
    for t in range(TPD):
        parts = [stats[k, t] for k in range(4)]
        top = functools.reduce(jnp.maximum, [p[0:1, :] for p in parts])
        total = jnp.zeros((1, TILE), jnp.float32)
        moment = jnp.zeros((1, TILE), jnp.float32)
        for p in parts:
            diff = p[0:1, :] - top
            scale = jnp.exp(diff)
            total = total + scale * p[1:2, :]
            moment = moment + scale * (p[2:3, :] + p[1:2, :] * diff)
        cert = 1.0 - (jnp.log(total) - moment / total) / jnp.log(jnp.float32(CLS))
        cert_ref[2 * t : 2 * t + 1, :] = cert[:, :HALF]
        cert_ref[2 * t + 1 : 2 * t + 2, :] = cert[:, HALF:]
        factor = jnp.exp(stats[y, t][0:1, :] - top) / total
        col = jnp.transpose(jnp.broadcast_to(factor, (8, TILE)), (1, 0))[:, 0:1]
        copies_in[t].wait()
        rows = slice(t * TILE, (t + 1) * TILE)
        outv[rows, :] = (ev[t] * col).astype(jnp.bfloat16)[:, :W]
        cp = pltpu.make_async_copy(
            outv.at[pl.ds(t * TILE, TILE)], pseudo_hbm.at[pl.ds(t * TILE, TILE)], sem_out.at[t]
        )
        cp.start()
        copies_out.append(cp)
    for cp in copies_out:
        cp.wait()


def local(prior, blocks, links, counts, fetch, seeds, inv_temp):
    bf, f32 = jnp.bfloat16, jnp.float32
    vmem = pltpu.VMEM
    expo, stats = pl.pallas_call(
        kernel,
        out_shape=(
            jax.ShapeDtypeStruct((TPD, TILE, TILE), f32),
            jax.ShapeDtypeStruct((4, TPD, 8, TILE), f32),
        ),
        in_specs=[
            pl.BlockSpec(memory_space=pltpu.SMEM),
            pl.BlockSpec(memory_space=pltpu.SMEM),
            pl.BlockSpec(memory_space=pltpu.VMEM),
            pl.BlockSpec(memory_space=pl.ANY),
            pl.BlockSpec(memory_space=pl.ANY),
            pl.BlockSpec(memory_space=pltpu.VMEM),
            pl.BlockSpec(memory_space=pltpu.VMEM),
        ],
        out_specs=(pl.BlockSpec(memory_space=pl.ANY), pl.BlockSpec(memory_space=pltpu.VMEM)),
        scratch_shapes=[
            vmem((TPD * TILE, W), bf),
            vmem((TPD, NB, TILE, TILE), bf),
            vmem((TPD, TILE, TILE), f32),
            vmem((TILE, TILE), f32),
            vmem((TPD, TILE, TILE), bf),
            vmem((TPD, TILE, TILE), bf),
            vmem((4, 7, 4, Q, TILE), bf),
            vmem((16, 8, 128), jnp.int32),
            pltpu.SMEM((16, 8, 128), jnp.int32),
            pltpu.SMEM((TPD * NB,), jnp.int32),
            pltpu.SMEM((TPD * NB,), jnp.int32),
            vmem((TPD, TILE, 1), jnp.int32),
            vmem((TPD, TILE, 1), f32),
            vmem((TPD, TILE, TILE), f32),
            vmem((4, TPD, 8, TILE), f32),
        ]
        + [vmem((3, TPD, Q, TILE), bf) for _ in range(8)]
        + [vmem((2, 4, Q, TILE), bf) for _ in range(8)]
        + [vmem((ZERO + 1, Q, TILE), bf) for _ in range(8)]
        + [
            pltpu.SemaphoreType.DMA((4, NAMES)),
            pltpu.SemaphoreType.DMA((8, NAMES)),
            pltpu.SemaphoreType.DMA((14,)),
            pltpu.SemaphoreType.DMA((14,)),
            pltpu.SemaphoreType.DMA((6,)),
            pltpu.SemaphoreType.DMA((6,)),
            pltpu.SemaphoreType.DMA((TPD,)),
            pltpu.SemaphoreType.DMA((10,)),
        ],
        compiler_params=pltpu.CompilerParams(
            collective_id=0, has_side_effects=True, vmem_limit_bytes=66_000_000
        ),
        name="propagate",
    )(
        links, counts, fetch.reshape(1, -1), prior, blocks,
        seeds.reshape(16, 128), inv_temp.reshape(16, 128),
    )
    pseudo, cert = pl.pallas_call(
        finish,
        out_shape=(
            jax.ShapeDtypeStruct((TPD * TILE, W), bf),
            jax.ShapeDtypeStruct((16, 128), f32),
        ),
        in_specs=[
            pl.BlockSpec(memory_space=pl.ANY),
            pl.BlockSpec(memory_space=pltpu.VMEM),
        ],
        out_specs=(pl.BlockSpec(memory_space=pl.ANY), pl.BlockSpec(memory_space=pltpu.VMEM)),
        scratch_shapes=[
            vmem((TPD, TILE, TILE), f32),
            vmem((TPD * TILE, W), bf),
            pltpu.SemaphoreType.DMA((TPD,)),
            pltpu.SemaphoreType.DMA((TPD,)),
        ],
        name="finish",
    )(expo, stats)
    return pseudo, cert.reshape(-1)


def solution(mesh):
    return jax.shard_map(
        local,
        mesh=mesh,
        in_specs=(
            P("rows", "cls"),
            P("rows", None, None, None),
            P("rows", None),
            P("rows"),
            P("rows", None, None),
            P("rows"),
            P("rows"),
        ),
        out_specs=(P("rows", "cls"), P("rows")),
        check_vma=False,
    )
```

```python
import functools
import math

import jax
import jax.numpy as jnp
from jax import lax
from jax.experimental import pallas as pl
from jax.experimental.pallas import tpu as pltpu
from jax.sharding import PartitionSpec as P

CLS = 1000
NB = 24
TPD = 8
TILE = 256
W = 250
HALF = 128
Q = 64
VLIM = 66_000_000
ZERO = 40

BLEND = 0.8
MESH = pl.DeviceIdType.MESH

GR, GL, FR, FL = (0, 1, 2, 3), (4, 5, 6, 7), (8, 9), (10, 11)
RR, RL, D0R, D1R, D0L, D1L, WR, WL, PT = range(12, 21)
NAMES = 21

PEERS = [(0, dz, dc) for dz in range(4) for dc in range(2) if (dz, dc) != (0, 0)] + [
    (dx, 0, dc) for dx in range(1, 4) for dc in range(2)
]


def kernel(
    links_hbm, counts_hbm, fetch_hbm, prior_hbm, blocks_hbm, seeds_hbm, temp_hbm,
    expo_hbm, stats_out,
    *scratch,
):
    (pv, bv, acc, raw, fld0, fld1, stage, frv, frm, tab_a, tab_b, seed_c, temp_r) = scratch[:13]
    expos, stats, seed_r = scratch[13:16]
    links_ref, counts_ref, fetch_ref, seeds_ref, temp_ref, small = scratch[-6:]
    gb = scratch[16:24]
    rl = scratch[24:32]
    cs = scratch[32:40]
    (send, recv, f_send, f_recv, y_send, y_recv, b_sem, loc) = scratch[40:-6]
    fld = (fld0, fld1)

    r = lax.axis_index("rows")
    y = lax.axis_index("cls")
    c = lax.rem(r, 2)
    x = lax.rem(r // 2, 4)
    z = r // 8

    def dev(dx, dz, dc):
        row = (lax.rem(z + dz, 4) * 4 + lax.rem(x + dx, 4)) * 2 + lax.rem(c + dc, 2)
        return (y, row)

    def idx(rnd, rt, kh):
        return (rnd * 2 + rt) * 2 + kh

    def step(rt, d, dc):
        return dev(0, d % 4, dc) if rt == 0 else dev(d % 4, 0, dc)

    def gstep(rt, d):
        return dev(d % 4, 0, 0) if rt == 0 else dev(0, d % 4, 0)

    block_cps = [
        pltpu.make_async_copy(blocks_hbm.at[t], bv.at[t], b_sem.at[t]) for t in range(TPD)
    ]
    barrier = pltpu.get_barrier_semaphore()
    for p in PEERS:
        pl.semaphore_signal(barrier, inc=1, device_id=dev(*p), device_id_type=MESH)
    for dy in range(1, 4):
        pl.semaphore_signal(
            barrier, inc=1, device_id=(lax.rem(y + dy, 4), r), device_id_type=MESH
        )
    prior_cp = pltpu.make_async_copy(prior_hbm, pv, loc.at[0])
    prior_cp.start()
    small_cps = [
        pltpu.make_async_copy(src, dst, small.at[k])
        for k, (src, dst) in enumerate(
            [
                (fetch_hbm, fetch_ref), (links_hbm, links_ref), (counts_hbm, counts_ref),
                (seeds_hbm, seeds_ref), (temp_hbm, temp_ref),
            ]
        )
    ]
    for cp in small_cps:
        cp.start()
    small_cps[0].wait()
    frv[0] = jnp.zeros((8, 128), jnp.int32)
    frv[0, 0:1, 0:32] = fetch_ref[...]
    frv[8] = jnp.zeros((8, 128), jnp.int32)
    frv[8, 0:1, 0:32] = fetch_ref[...]
    prior_cp.wait()
    for t in range(TPD):
        fld0[t, :, HALF:] = jnp.zeros((TILE, HALF), jnp.bfloat16)
        fld0[t, :, :W] = pv[t * TILE : (t + 1) * TILE, :]
    pl.semaphore_wait(barrier, len(PEERS) + 3)

    def g_copy(rnd, rt, kh, name):
        i = idx(rnd, rt, kh)
        rows = pl.ds(kh * HALF + rt * Q, Q)
        if name in GR or name in GL:
            pair = pl.ds(2 * (name % 4), 2)
            d, far = (1, 2) if name in GR else (-1, 0)
            src, dst = fld[rnd].at[pair, rows, :], gb[i].at[far, pair]
        else:
            d, far = (1, 2) if name in FR else (-1, 0)
            pair = pl.ds(2 * (name - 8), 2)
            src, dst = gb[i].at[far, pair], gb[i].at[1, pair]
        return pltpu.make_async_remote_copy(
            src_ref=src, dst_ref=dst, send_sem=send.at[idx(0, rt, kh), name],
            recv_sem=recv.at[i, name], device_id=gstep(rt, d), device_id_type=MESH,
        )

    def p_copy(rnd, rt, kh, name):
        i = idx(rnd, rt, kh)
        s = idx(0, rt, kh)
        group = lambda g: stage.at[s, g]
        slot = lambda d, dc: cs[i].at[pl.ds((d * 2 + dc) * 4, 4)]
        src, dst, d, dc = {
            RR: (group(2), rl[i].at[0], 1, 0),
            RL: (group(3), rl[i].at[1], -1, 0),
            D0R: (group(0), slot(3, 0), 1, 0),
            D1R: (group(1), slot(3, 1), 1, 1),
            D0L: (group(4), slot(1, 0), -1, 0),
            D1L: (group(5), slot(1, 1), -1, 1),
            WR: (rl[i].at[0], slot(2, 0), 1, 0),
            WL: (rl[i].at[1], slot(2, 1), -1, 1),
            PT: (group(6), slot(0, 1), 0, 1),
        }[name]
        return pltpu.make_async_remote_copy(
            src_ref=src, dst_ref=dst, send_sem=send.at[s, name],
            recv_sem=recv.at[i, name], device_id=step(rt, d, dc), device_id_type=MESH,
        )

    def start_g(rnd, kh, names):
        for name in names:
            for rt in range(2):
                g_copy(rnd, rt, kh, name).start()

    def wait_g(rnd, kh, names):
        for name in names:
            for rt in range(2):
                g_copy(rnd, rt, kh, name).wait_recv()

    def start_p(rnd, kh, names):
        for name in names:
            for rt in range(2):
                p_copy(rnd, rt, kh, name).start()

    def wait_p(rnd, kh, names):
        for name in names:
            for rt in range(2):
                p_copy(rnd, rt, kh, name).wait_recv()

    def wait_sends(kh, rnd):
        for rt in range(2):
            for name in GR + GL + FR + FL:
                g_copy(rnd, rt, kh, name).wait_send()
            for name in (RR, RL, D0R, D1R, D0L, D1L, WR, WL, PT):
                p_copy(rnd, rt, kh, name).wait_send()

    f_copies = []
    for k, (dx, dz, dc, base) in enumerate(
        [(0, dz, dc, 0) for dz in range(4) for dc in range(2) if (dz, dc) != (0, 0)]
        + [(dx, 0, dc, 8) for dx in range(4) for dc in range(2) if (dx, dc) != (0, 0)]
    ):
        d = dz if base == 0 else dx
        f_copies.append(
            pltpu.make_async_remote_copy(
                src_ref=frv.at[0], dst_ref=frv.at[base + ((4 - d) % 4) * 2 + dc],
                send_sem=f_send.at[k], recv_sem=f_recv.at[k],
                device_id=dev(dx, dz, dc), device_id_type=MESH,
            )
        )

    def src_row(rt, d):
        if rt == 0:
            return (z * 4 + lax.rem(x + d, 4)) * 2 + c
        return (lax.rem(z + d, 4) * 4 + x) * 2 + c

    def select(rnd, kh):
        for rt in range(2):
            i = idx(rnd, rt, kh)
            rows = pl.ds(kh * HALF + rt * Q, Q)
            for d in range(4):
                row = src_row(rt, d)
                for dd in (2, 1, 3, 0):
                    for dc in range(2):
                        f = frm[rt * 8 + dd * 2 + dc, 0, row]
                        value = fld[rnd][f, rows, :] if d == 0 else gb[i][d - 1, f]
                        if (dd, dc) == (0, 0):
                            cs[i][d] = value
                        else:
                            g = 6 if dd == 0 else (dd - 1) * 2 + dc
                            stage[idx(0, rt, kh), g, d] = value

    def own_slots(rnd, t):
        for rt in range(2):
            for kh in range(2):
                a = kh * HALF + rt * Q
                cs[idx(rnd, rt, kh)][4 * TPD + t] = fld[rnd][t, a : a + Q, :]

    def product(rnd, kh, t):
        a = idx(rnd, 0, kh)
        b = idx(rnd, 1, kh)
        total = None
        for jp in range(NB // 2):
            left, right = [], []
            for j in (2 * jp, 2 * jp + 1):
                left.append(bv[t, j, :, kh * HALF : (kh + 1) * HALF])
                right.append(cs[a][tab_a[t * NB + j]])
                right.append(cs[b][tab_b[t * NB + j]])
            d = jnp.dot(
                jnp.concatenate(left, axis=1), jnp.concatenate(right, axis=0),
                preferred_element_type=jnp.float32,
            )
            total = d if total is None else total + d
        return total

    lane = lax.broadcasted_iota(jnp.int32, (TILE, TILE), 1)
    inside = lane < W
    column = lane + y * W

    def mixed(t, total):
        hit = (seed_c[t] == column) & inside
        return BLEND * total + jnp.where(hit, jnp.float32(1.0 - BLEND), jnp.float32(0.0))

    HOP = ((GR[0], GL[0]), (GR[2], GL[2]), (GR[1], GL[1]), (GR[3], GL[3]))
    ALL_HOPS = sum(HOP, ())
    GO_ON = (((GR[0], FR[0]), (GL[2], FL[0])), ((GR[1], FR[1]), (GL[3], FL[1])))
    REST = (GR[2], GR[3], GL[0], GL[1]) + FR + FL
    SENDS = (RR, RL, D0R, D0L, D1R, D1L, PT)
    RELAY = (WR, WL)
    FINAL = (D0R, D0L, D1R, D1L, PT, WR, WL)

    for cp in f_copies:
        cp.start()
    start_g(0, 0, ALL_HOPS)
    for cp in block_cps:
        cp.start()

    for rnd in range(2):
        for rt in range(2):
            for kh in range(2):
                cs[idx(rnd, rt, kh)][ZERO] = jnp.zeros((Q, TILE), jnp.bfloat16)
    for t in range(TPD):
        own_slots(0, t)

    def forward(rnd, kh):
        for part in GO_ON:
            for name, onward in part:
                wait_g(rnd, kh, (name,))
                start_g(rnd, kh, (onward,))

    def prepare():
        for cp in small_cps[1:]:
            cp.wait()
        seeds_t = jnp.transpose(seeds_ref[...].astype(jnp.float32), (1, 0))
        for t in range(TPD):
            for h in range(2):
                k = 2 * t + h
                seed_c[t, h * HALF : (h + 1) * HALF, :] = seeds_t[:, k : k + 1].astype(jnp.int32)
                half = slice(h * HALF, (h + 1) * HALF)
                seed_r[t : t + 1, half] = seeds_ref[k : k + 1, :]
                temp_r[t : t + 1, half] = temp_ref[k : k + 1, :]
        for cp in f_copies:
            cp.wait()
        to_smem = pltpu.make_async_copy(frv, frm, loc.at[1])
        to_smem.start()

        def slots(t, carry):
            count = counts_ref[t]
            for j in range(NB):
                v = links_ref[t, j]
                s = jnp.maximum(v - TPD, 0)
                dz = ((s >> 3) + 4 - z) & 3
                dx = (((s >> 1) & 3) + 4 - x) & 3
                dc = (s + c) & 1
                own = v < TPD
                live = j < count
                sa = jnp.where(own, 4 * TPD + v, (dz * 2 + dc) * 4 + dx)
                sb = jnp.where(own, 4 * TPD + v, (dx * 2 + dc) * 4 + dz)
                tab_a[t * NB + j] = jnp.where(live, sa, ZERO)
                tab_b[t * NB + j] = jnp.where(live, sb, ZERO)
            return carry

        lax.fori_loop(0, TPD, slots, 0)
        to_smem.wait()

    def exchange(rnd):
        forward(rnd, 0)
        start_g(rnd, 1, ALL_HOPS)
        if rnd == 0:
            prepare()
        wait_g(rnd, 0, REST)
        select(rnd, 0)
        forward(rnd, 1)
        start_p(rnd, 0, SENDS)
        wait_g(rnd, 1, REST)
        select(rnd, 1)
        wait_p(rnd, 0, (RR, RL))
        start_p(rnd, 0, RELAY)
        start_p(rnd, 1, SENDS)
        wait_p(rnd, 0, FINAL)

    def first_chunk(rnd):
        def body(t, carry):
            @pl.when(t == 4)
            def _():
                wait_p(rnd, 1, (RR, RL))
                start_p(rnd, 1, RELAY)

            acc[t] = product(rnd, 0, t)
            return carry

        lax.fori_loop(0, TPD, body, 0)
        wait_p(rnd, 1, FINAL)

    exchange(0)
    for cp in block_cps:
        cp.wait()
    first_chunk(0)
    for kh in range(2):
        wait_sends(kh, 0)

    def first_tile(i, carry):
        for k in range(3):

            @pl.when(i == 2 * k + 2)
            def _():
                start_g(1, 0, HOP[k])

        t = (i // 4) * 2 + ((i // 2) % 2) * 4 + i % 2
        value = mixed(t, acc[t] + product(0, 1, t)).astype(jnp.bfloat16)
        fld1[t] = value
        for rt in range(2):
            for kh in range(2):
                a = kh * HALF + rt * Q
                cs[idx(1, rt, kh)][4 * TPD + t] = value[a : a + Q, :]
        return carry

    lax.fori_loop(0, TPD, first_tile, 0)
    start_g(1, 0, HOP[3])

    exchange(1)
    first_chunk(1)

    class_no = lax.broadcasted_iota(jnp.int32, (TILE, TILE), 0)
    real = class_no < W
    class_no = class_no + y * W

    def softmax(t):
        total = jnp.transpose(raw[...], (1, 0))
        hit = (seed_r[pl.ds(t, 1), :] == class_no) & real
        total = BLEND * total + jnp.where(hit, jnp.float32(1.0 - BLEND), jnp.float32(0.0))
        logits = temp_r[pl.ds(t, 1), :] * total
        top = jnp.max(jnp.where(real, logits, -jnp.inf), axis=0, keepdims=True)
        shifted = jnp.where(real, logits - top, 0.0)
        expo = jnp.where(real, jnp.exp(shifted), 0.0)
        return expo, (
            top,
            jnp.sum(expo, axis=0, keepdims=True),
            jnp.sum(expo * shifted, axis=0, keepdims=True),
        )

    def keep(t, expo, stat):
        expos[t] = jnp.transpose(expo, (1, 0)).astype(jnp.bfloat16)
        for k in range(3):
            stats[y, k, pl.ds(t, 1), :] = stat[k]

    def y_copy(dy, slot):
        return pltpu.make_async_remote_copy(
            src_ref=stats.at[y], dst_ref=stats.at[slot],
            send_sem=y_send.at[dy - 1], recv_sem=y_recv.at[dy - 1],
            device_id=(lax.rem(y + dy, 4), r), device_id_type=MESH,
        )

    def out_copy(t):
        return pltpu.make_async_copy(expos.at[t], expo_hbm.at[t], loc.at[2 + t])

    def last_tile(t, carry):
        before = jnp.maximum(t - 1, 0)
        expo, stat = softmax(before)
        total = acc[t] + product(1, 1, t)
        keep(before, expo, stat)
        raw[...] = total

        @pl.when(t == 5)
        def _():
            for k in range(4):
                out_copy(k).start()

        return carry

    raw[...] = jnp.zeros((TILE, TILE), jnp.float32)
    lax.fori_loop(0, TPD, last_tile, 0)
    keep(TPD - 1, *softmax(TPD - 1))
    for dy in (2, 1, 3):
        y_copy(dy, y).start()
    for k in range(4, TPD):
        out_copy(k).start()
    for kh in range(2):
        wait_sends(kh, 1)
    for k in range(TPD):
        out_copy(k).wait()
    for dy in range(1, 4):
        y_copy(dy, y).wait_send()
        y_copy(dy, lax.rem(y + 4 - dy, 4)).wait_recv()
    stats_cp = pltpu.make_async_copy(stats, stats_out, loc.at[1])
    stats_cp.start()
    stats_cp.wait()


def finish(expo_hbm, stats_hbm, pseudo_hbm, cert_ref, ev, outv, stats, sem_in, sem_out):
    y = lax.axis_index("cls")
    stats_cp = pltpu.make_async_copy(stats_hbm, stats, sem_in.at[TPD])
    stats_cp.start()
    copies_in, copies_out = [], []
    for t in range(TPD):
        cp = pltpu.make_async_copy(expo_hbm.at[t], ev.at[t], sem_in.at[t])
        cp.start()
        copies_in.append(cp)
    stats_cp.wait()
    top = functools.reduce(jnp.maximum, [stats[k, 0] for k in range(4)])
    total = jnp.zeros((TPD, TILE), jnp.float32)
    moment = jnp.zeros((TPD, TILE), jnp.float32)
    for k in range(4):
        diff = stats[k, 0] - top
        scale = jnp.exp(diff)
        total = total + scale * stats[k, 1]
        moment = moment + scale * (stats[k, 2] + stats[k, 1] * diff)
    factor = jnp.transpose(jnp.exp(stats[y, 0] - top) / total, (1, 0))
    for t in range(TPD):
        copies_in[t].wait()
        rows = slice(t * TILE, (t + 1) * TILE)
        part = ev[t].astype(jnp.float32) * factor[:, t : t + 1]
        outv[rows, :] = part.astype(jnp.bfloat16)[:, :W]
        cp = pltpu.make_async_copy(
            outv.at[pl.ds(t * TILE, TILE)], pseudo_hbm.at[pl.ds(t * TILE, TILE)], sem_out.at[t]
        )
        cp.start()
        copies_out.append(cp)
    cert = 1.0 - (jnp.log(total) - moment / total) / jnp.log(jnp.float32(CLS))
    for t in range(TPD):
        cert_ref[2 * t : 2 * t + 1, :] = cert[t : t + 1, :HALF]
        cert_ref[2 * t + 1 : 2 * t + 2, :] = cert[t : t + 1, HALF:]
    for cp in copies_out:
        cp.wait()


def local(prior, blocks, links, counts, fetch, seeds, inv_temp):
    bf, f32 = jnp.bfloat16, jnp.float32
    vmem = pltpu.VMEM
    expo, stats = pl.pallas_call(
        kernel,
        out_shape=(
            jax.ShapeDtypeStruct((TPD, TILE, TILE), bf),
            jax.ShapeDtypeStruct((4, 3, TPD, TILE), f32),
        ),
        in_specs=[pl.BlockSpec(memory_space=pl.ANY)] * 7,
        out_specs=(pl.BlockSpec(memory_space=pl.ANY), pl.BlockSpec(memory_space=pl.ANY)),
        scratch_shapes=[
            vmem((TPD * TILE, W), bf),
            vmem((TPD, NB, TILE, TILE), bf),
            vmem((TPD, TILE, TILE), f32),
            vmem((TILE, TILE), f32),
            vmem((TPD, TILE, TILE), bf),
            vmem((TPD, TILE, TILE), bf),
            vmem((4, 7, 4, Q, TILE), bf),
            vmem((16, 8, 128), jnp.int32),
            pltpu.SMEM((16, 8, 128), jnp.int32),
            pltpu.SMEM((TPD * NB,), jnp.int32),
            pltpu.SMEM((TPD * NB,), jnp.int32),
            vmem((TPD, TILE, 1), jnp.int32),
            vmem((TPD, TILE), f32),
            vmem((TPD, TILE, TILE), bf),
            vmem((4, 3, TPD, TILE), f32),
            vmem((TPD, TILE), jnp.int32),
        ]
        + [vmem((3, TPD, Q, TILE), bf) for _ in range(8)]
        + [vmem((2, 4, Q, TILE), bf) for _ in range(8)]
        + [vmem((ZERO + 1, Q, TILE), bf) for _ in range(8)]
        + [
            pltpu.SemaphoreType.DMA((4, NAMES)),
            pltpu.SemaphoreType.DMA((8, NAMES)),
            pltpu.SemaphoreType.DMA((14,)),
            pltpu.SemaphoreType.DMA((14,)),
            pltpu.SemaphoreType.DMA((3,)),
            pltpu.SemaphoreType.DMA((3,)),
            pltpu.SemaphoreType.DMA((TPD,)),
            pltpu.SemaphoreType.DMA((10,)),
            pltpu.SMEM((TPD, NB), jnp.int32),
            pltpu.SMEM((TPD,), jnp.int32),
            vmem((1, 32), jnp.int32),
            vmem((16, 128), jnp.int32),
            vmem((16, 128), f32),
            pltpu.SemaphoreType.DMA((5,)),
        ],
        compiler_params=pltpu.CompilerParams(
            collective_id=0, has_side_effects=True, vmem_limit_bytes=VLIM
        ),
        name="propagate",
    )(
        links, counts, fetch.reshape(1, -1), prior, blocks,
        seeds.reshape(16, 128), inv_temp.reshape(16, 128),
    )
    pseudo, cert = pl.pallas_call(
        finish,
        out_shape=(
            jax.ShapeDtypeStruct((TPD * TILE, W), bf),
            jax.ShapeDtypeStruct((16, 128), f32),
        ),
        in_specs=[
            pl.BlockSpec(memory_space=pl.ANY),
            pl.BlockSpec(memory_space=pl.ANY),
        ],
        out_specs=(pl.BlockSpec(memory_space=pl.ANY), pl.BlockSpec(memory_space=pltpu.VMEM)),
        scratch_shapes=[
            vmem((TPD, TILE, TILE), bf),
            vmem((TPD * TILE, W), bf),
            vmem((4, 3, TPD, TILE), f32),
            pltpu.SemaphoreType.DMA((TPD + 1,)),
            pltpu.SemaphoreType.DMA((TPD,)),
        ],
        name="finish",
    )(expo, stats)
    return pseudo, cert.reshape(-1)


def solution(mesh):
    return jax.shard_map(
        local,
        mesh=mesh,
        in_specs=(
            P("rows", "cls"),
            P("rows", None, None, None),
            P("rows", None),
            P("rows"),
            P("rows", None, None),
            P("rows"),
            P("rows"),
        ),
        out_specs=(P("rows", "cls"), P("rows")),
        check_vma=False,
    )
```

```python
import functools
import math

import jax
import jax.numpy as jnp
from jax import lax
from jax.experimental import pallas as pl
from jax.experimental.pallas import tpu as pltpu
from jax.sharding import PartitionSpec as P

CLS = 1000
NB = 24
TPD = 8
TILE = 256
W = 250
HALF = 128
Q = 64
VLIM = 66_000_000
ZERO = 40

BLEND = 0.8
MESH = pl.DeviceIdType.MESH

GR, GL, FR, FL = (0, 1, 2, 3), (4, 5, 6, 7), (8, 9), (10, 11)
RR, RL, D0R, D1R, D0L, D1L, WR, WL, PT = range(12, 21)
GR1, GL1 = 21, 22
NAMES = 23

PEERS = [(0, dz, dc) for dz in range(4) for dc in range(2) if (dz, dc) != (0, 0)] + [
    (dx, 0, dc) for dx in range(1, 4) for dc in range(2)
]


def kernel(
    links_hbm, counts_hbm, fetch_hbm, prior_hbm, blocks_hbm, seeds_hbm, temp_hbm,
    expo_hbm, stats_out,
    *scratch,
):
    (pv, bv, acc, raw, fld0, fld1, stage, frv, frm, tab_a, tab_b, seed_c, temp_r) = scratch[:13]
    expos, stats, seed_r = scratch[13:16]
    links_ref, counts_ref, fetch_ref, seeds_ref, temp_ref, small = scratch[-6:]
    gb = scratch[16:24]
    rl = scratch[24:32]
    cs = scratch[32:40]
    (send, recv, f_send, f_recv, y_send, y_recv, b_sem, loc) = scratch[40:-6]
    fld = (fld0, fld1)

    r = lax.axis_index("rows")
    y = lax.axis_index("cls")
    c = lax.rem(r, 2)
    x = lax.rem(r // 2, 4)
    z = r // 8

    def dev(dx, dz, dc):
        row = (lax.rem(z + dz, 4) * 4 + lax.rem(x + dx, 4)) * 2 + lax.rem(c + dc, 2)
        return (y, row)

    def idx(rnd, rt, kh):
        return (rnd * 2 + rt) * 2 + kh

    def step(rt, d, dc):
        return dev(0, d % 4, dc) if rt == 0 else dev(d % 4, 0, dc)

    def gstep(rt, d):
        return dev(d % 4, 0, 0) if rt == 0 else dev(0, d % 4, 0)

    block_cps = [
        pltpu.make_async_copy(blocks_hbm.at[t], bv.at[t], b_sem.at[t]) for t in range(TPD)
    ]
    barrier = pltpu.get_barrier_semaphore()
    for p in PEERS:
        pl.semaphore_signal(barrier, inc=1, device_id=dev(*p), device_id_type=MESH)
    for dy in range(1, 4):
        pl.semaphore_signal(
            barrier, inc=1, device_id=(lax.rem(y + dy, 4), r), device_id_type=MESH
        )
    prior_cp = pltpu.make_async_copy(prior_hbm, pv, loc.at[0])
    prior_cp.start()
    small_cps = [
        pltpu.make_async_copy(src, dst, small.at[k])
        for k, (src, dst) in enumerate(
            [
                (fetch_hbm, fetch_ref), (links_hbm, links_ref), (counts_hbm, counts_ref),
                (seeds_hbm, seeds_ref), (temp_hbm, temp_ref),
            ]
        )
    ]
    for cp in small_cps:
        cp.start()
    small_cps[0].wait()
    frv[0] = jnp.zeros((8, 128), jnp.int32)
    frv[0, 0:1, 0:32] = fetch_ref[...]
    frv[8] = jnp.zeros((8, 128), jnp.int32)
    frv[8, 0:1, 0:32] = fetch_ref[...]
    prior_cp.wait()
    for t in range(TPD):
        fld0[t, :, HALF:] = jnp.zeros((TILE, HALF), jnp.bfloat16)
        fld0[t, :, :W] = pv[t * TILE : (t + 1) * TILE, :]
    pl.semaphore_wait(barrier, len(PEERS) + 3)

    def g_copy(rnd, rt, kh, name):
        i = idx(rnd, rt, kh)
        rows = pl.ds(kh * HALF + rt * Q, Q)
        if name in GR or name in GL:
            k = name % 4
            pair = pl.ds(2 * k, 2) if k else pl.ds(0, 1)
            d, far = (1, 2) if name in GR else (-1, 0)
            src, dst = fld[rnd].at[pair, rows, :], gb[i].at[far, pair]
        elif name in (GR1, GL1):
            pair = pl.ds(1, 1)
            d, far = (1, 2) if name == GR1 else (-1, 0)
            src, dst = fld[rnd].at[pair, rows, :], gb[i].at[far, pair]
        else:
            d, far = (1, 2) if name in FR else (-1, 0)
            pair = pl.ds(2 * (name - 8), 2)
            src, dst = gb[i].at[far, pair], gb[i].at[1, pair]
        return pltpu.make_async_remote_copy(
            src_ref=src, dst_ref=dst, send_sem=send.at[idx(0, rt, kh), name],
            recv_sem=recv.at[i, name], device_id=gstep(rt, d), device_id_type=MESH,
        )

    def p_copy(rnd, rt, kh, name):
        i = idx(rnd, rt, kh)
        s = idx(0, rt, kh)
        group = lambda g: stage.at[s, g]
        slot = lambda d, dc: cs[i].at[pl.ds((d * 2 + dc) * 4, 4)]
        src, dst, d, dc = {
            RR: (group(2), rl[i].at[0], 1, 0),
            RL: (group(3), rl[i].at[1], -1, 0),
            D0R: (group(0), slot(3, 0), 1, 0),
            D1R: (group(1), slot(3, 1), 1, 1),
            D0L: (group(4), slot(1, 0), -1, 0),
            D1L: (group(5), slot(1, 1), -1, 1),
            WR: (rl[i].at[0], slot(2, 0), 1, 0),
            WL: (rl[i].at[1], slot(2, 1), -1, 1),
            PT: (group(6), slot(0, 1), 0, 1),
        }[name]
        return pltpu.make_async_remote_copy(
            src_ref=src, dst_ref=dst, send_sem=send.at[s, name],
            recv_sem=recv.at[i, name], device_id=step(rt, d, dc), device_id_type=MESH,
        )

    def start_g(rnd, kh, names):
        for name in names:
            for rt in range(2):
                g_copy(rnd, rt, kh, name).start()

    def wait_g(rnd, kh, names):
        for name in names:
            for rt in range(2):
                g_copy(rnd, rt, kh, name).wait_recv()

    def start_p(rnd, kh, names):
        for name in names:
            for rt in range(2):
                p_copy(rnd, rt, kh, name).start()

    def wait_p(rnd, kh, names):
        for name in names:
            for rt in range(2):
                p_copy(rnd, rt, kh, name).wait_recv()

    def wait_sends(kh, rnd):
        for rt in range(2):
            for name in GR + GL + FR + FL + (GR1, GL1):
                g_copy(rnd, rt, kh, name).wait_send()
            for name in (RR, RL, D0R, D1R, D0L, D1L, WR, WL, PT):
                p_copy(rnd, rt, kh, name).wait_send()

    f_copies = []
    for k, (dx, dz, dc, base) in enumerate(
        [(0, dz, dc, 0) for dz in range(4) for dc in range(2) if (dz, dc) != (0, 0)]
        + [(dx, 0, dc, 8) for dx in range(4) for dc in range(2) if (dx, dc) != (0, 0)]
    ):
        d = dz if base == 0 else dx
        f_copies.append(
            pltpu.make_async_remote_copy(
                src_ref=frv.at[0], dst_ref=frv.at[base + ((4 - d) % 4) * 2 + dc],
                send_sem=f_send.at[k], recv_sem=f_recv.at[k],
                device_id=dev(dx, dz, dc), device_id_type=MESH,
            )
        )

    def src_row(rt, d):
        if rt == 0:
            return (z * 4 + lax.rem(x + d, 4)) * 2 + c
        return (lax.rem(z + d, 4) * 4 + x) * 2 + c

    def select(rnd, kh):
        for rt in range(2):
            i = idx(rnd, rt, kh)
            rows = pl.ds(kh * HALF + rt * Q, Q)
            for d in range(4):
                row = src_row(rt, d)
                for dd in (2, 1, 3, 0):
                    for dc in range(2):
                        f = frm[rt * 8 + dd * 2 + dc, 0, row]
                        value = fld[rnd][f, rows, :] if d == 0 else gb[i][d - 1, f]
                        if (dd, dc) == (0, 0):
                            cs[i][d] = value
                        else:
                            g = 6 if dd == 0 else (dd - 1) * 2 + dc
                            stage[idx(0, rt, kh), g, d] = value

    def own_slots(rnd, t):
        for rt in range(2):
            for kh in range(2):
                a = kh * HALF + rt * Q
                cs[idx(rnd, rt, kh)][4 * TPD + t] = fld[rnd][t, a : a + Q, :]

    def product(rnd, kh, t):
        a = idx(rnd, 0, kh)
        b = idx(rnd, 1, kh)
        total = None
        for jp in range(NB // 2):
            left, right = [], []
            for j in (2 * jp, 2 * jp + 1):
                left.append(bv[t, j, :, kh * HALF : (kh + 1) * HALF])
                right.append(cs[a][tab_a[t * NB + j]])
                right.append(cs[b][tab_b[t * NB + j]])
            d = jnp.dot(
                jnp.concatenate(left, axis=1), jnp.concatenate(right, axis=0),
                preferred_element_type=jnp.float32,
            )
            total = d if total is None else total + d
        return total

    lane = lax.broadcasted_iota(jnp.int32, (TILE, TILE), 1)
    inside = lane < W
    column = lane + y * W

    def mixed(t, total):
        hit = (seed_c[t] == column) & inside
        return BLEND * total + jnp.where(hit, jnp.float32(1.0 - BLEND), jnp.float32(0.0))

    HOP = ((GR1, GL1), (GR[2], GL[2]), (GR[1], GL[1]), (GR[3], GL[3]))
    ALL_HOPS = (GR[0], GL[0]) + sum(HOP, ())
    GO_ON = (((GR1, FR[0]), (GL[2], FL[0])), ((GR[1], FR[1]), (GL[3], FL[1])))
    REST = (GR[2], GR[3], GL[0], GL1, GL[1]) + FR + FL
    SENDS = (RR, RL, D0R, D0L, D1R, D1L, PT)
    RELAY = (WR, WL)
    FINAL = (D0R, D0L, D1R, D1L, PT, WR, WL)

    for cp in f_copies:
        cp.start()
    start_g(0, 0, ALL_HOPS)
    for cp in block_cps:
        cp.start()

    def forward(rnd, kh):
        wait_g(rnd, kh, (GR[0],))
        for part in GO_ON:
            for name, onward in part:
                wait_g(rnd, kh, (name,))
                start_g(rnd, kh, (onward,))

    def prepare():
        for cp in f_copies:
            cp.wait()
        to_smem = pltpu.make_async_copy(frv, frm, loc.at[1])
        to_smem.start()
        to_smem.wait()

    def prepare_rest():
        for rn in range(2):
            for rt in range(2):
                for kh in range(2):
                    cs[idx(rn, rt, kh)][ZERO] = jnp.zeros((Q, TILE), jnp.bfloat16)
        for t in range(TPD):
            own_slots(0, t)
        for cp in small_cps[1:]:
            cp.wait()
        seeds_t = jnp.transpose(seeds_ref[...].astype(jnp.float32), (1, 0))
        for t in range(TPD):
            for h in range(2):
                k = 2 * t + h
                seed_c[t, h * HALF : (h + 1) * HALF, :] = seeds_t[:, k : k + 1].astype(jnp.int32)
                half = slice(h * HALF, (h + 1) * HALF)
                seed_r[t : t + 1, half] = seeds_ref[k : k + 1, :]
                temp_r[t : t + 1, half] = temp_ref[k : k + 1, :]

        def slots(t, carry):
            count = counts_ref[t]
            for j in range(NB):
                v = links_ref[t, j]
                s = jnp.maximum(v - TPD, 0)
                dz = ((s >> 3) + 4 - z) & 3
                dx = (((s >> 1) & 3) + 4 - x) & 3
                dc = (s + c) & 1
                own = v < TPD
                live = j < count
                sa = jnp.where(own, 4 * TPD + v, (dz * 2 + dc) * 4 + dx)
                sb = jnp.where(own, 4 * TPD + v, (dx * 2 + dc) * 4 + dz)
                tab_a[t * NB + j] = jnp.where(live, sa, ZERO)
                tab_b[t * NB + j] = jnp.where(live, sb, ZERO)
            return carry

        lax.fori_loop(0, TPD, slots, 0)

    def exchange(rnd):
        forward(rnd, 0)
        start_g(rnd, 1, ALL_HOPS)
        if rnd == 0:
            prepare()
        wait_g(rnd, 0, REST)
        select(rnd, 0)
        forward(rnd, 1)
        start_p(rnd, 0, SENDS)
        wait_g(rnd, 1, REST)
        select(rnd, 1)
        wait_p(rnd, 0, (RR, RL))
        start_p(rnd, 0, RELAY)
        start_p(rnd, 1, SENDS)
        if rnd == 0:
            prepare_rest()
        wait_p(rnd, 0, FINAL)

    def first_chunk(rnd):
        def body(t, carry):
            @pl.when(t == 4)
            def _():
                wait_p(rnd, 1, (RR, RL))
                start_p(rnd, 1, RELAY)

            acc[t] = product(rnd, 0, t)
            return carry

        lax.fori_loop(0, TPD, body, 0)
        wait_p(rnd, 1, FINAL)

    exchange(0)
    for cp in block_cps:
        cp.wait()
    first_chunk(0)
    for kh in range(2):
        wait_sends(kh, 0)

    def first_tile(i, carry):
        @pl.when(i == 1)
        def _():
            start_g(1, 0, (GR[0], GL[0]))

        for k in range(3):

            @pl.when(i == 2 * k + 2)
            def _():
                start_g(1, 0, HOP[k])

        t = (i // 4) * 2 + ((i // 2) % 2) * 4 + i % 2
        value = mixed(t, acc[t] + product(0, 1, t)).astype(jnp.bfloat16)
        fld1[t] = value
        for rt in range(2):
            for kh in range(2):
                a = kh * HALF + rt * Q
                cs[idx(1, rt, kh)][4 * TPD + t] = value[a : a + Q, :]
        return carry

    lax.fori_loop(0, TPD, first_tile, 0)
    start_g(1, 0, HOP[3])

    exchange(1)
    first_chunk(1)

    class_no = lax.broadcasted_iota(jnp.int32, (TILE, TILE), 0)
    real = class_no < W
    class_no = class_no + y * W

    def softmax(t):
        total = jnp.transpose(raw[...], (1, 0))
        hit = (seed_r[pl.ds(t, 1), :] == class_no) & real
        total = BLEND * total + jnp.where(hit, jnp.float32(1.0 - BLEND), jnp.float32(0.0))
        logits = temp_r[pl.ds(t, 1), :] * total
        top = jnp.max(jnp.where(real, logits, -jnp.inf), axis=0, keepdims=True)
        shifted = jnp.where(real, logits - top, 0.0)
        expo = jnp.where(real, jnp.exp(shifted), 0.0)
        return expo, (
            top,
            jnp.sum(expo, axis=0, keepdims=True),
            jnp.sum(expo * shifted, axis=0, keepdims=True),
        )

    def keep(t, expo, stat):
        expos[t] = jnp.transpose(expo, (1, 0)).astype(jnp.bfloat16)
        for k in range(3):
            stats[y, k, pl.ds(t, 1), :] = stat[k]

    def y_copy(dy, slot):
        return pltpu.make_async_remote_copy(
            src_ref=stats.at[y], dst_ref=stats.at[slot],
            send_sem=y_send.at[dy - 1], recv_sem=y_recv.at[dy - 1],
            device_id=(lax.rem(y + dy, 4), r), device_id_type=MESH,
        )

    def out_copy(t):
        return pltpu.make_async_copy(expos.at[t], expo_hbm.at[t], loc.at[2 + t])

    def last_tile(t, carry):
        before = jnp.maximum(t - 1, 0)
        expo, stat = softmax(before)
        total = acc[t] + product(1, 1, t)
        keep(before, expo, stat)
        raw[...] = total

        @pl.when(t == 5)
        def _():
            for k in range(4):
                out_copy(k).start()

        return carry

    raw[...] = jnp.zeros((TILE, TILE), jnp.float32)
    lax.fori_loop(0, TPD, last_tile, 0)
    keep(TPD - 1, *softmax(TPD - 1))
    for dy in (2, 1, 3):
        y_copy(dy, y).start()
    for k in range(4, TPD):
        out_copy(k).start()
    for kh in range(2):
        wait_sends(kh, 1)
    for k in range(TPD):
        out_copy(k).wait()
    for dy in range(1, 4):
        y_copy(dy, y).wait_send()
        y_copy(dy, lax.rem(y + 4 - dy, 4)).wait_recv()
    stats_cp = pltpu.make_async_copy(stats, stats_out, loc.at[1])
    stats_cp.start()
    stats_cp.wait()


def finish(expo_hbm, stats_hbm, pseudo_hbm, cert_ref, ev, outv, stats, sem_in, sem_out):
    y = lax.axis_index("cls")
    stats_cp = pltpu.make_async_copy(stats_hbm, stats, sem_in.at[TPD])
    stats_cp.start()
    copies_in, copies_out = [], []
    for t in range(TPD):
        cp = pltpu.make_async_copy(expo_hbm.at[t], ev.at[t], sem_in.at[t])
        cp.start()
        copies_in.append(cp)
    stats_cp.wait()
    top = functools.reduce(jnp.maximum, [stats[k, 0] for k in range(4)])
    total = jnp.zeros((TPD, TILE), jnp.float32)
    moment = jnp.zeros((TPD, TILE), jnp.float32)
    for k in range(4):
        diff = stats[k, 0] - top
        scale = jnp.exp(diff)
        total = total + scale * stats[k, 1]
        moment = moment + scale * (stats[k, 2] + stats[k, 1] * diff)
    factor = jnp.transpose(jnp.exp(stats[y, 0] - top) / total, (1, 0))
    for t in range(TPD):
        copies_in[t].wait()
        rows = slice(t * TILE, (t + 1) * TILE)
        part = ev[t].astype(jnp.float32) * factor[:, t : t + 1]
        outv[rows, :] = part.astype(jnp.bfloat16)[:, :W]
        cp = pltpu.make_async_copy(
            outv.at[pl.ds(t * TILE, TILE)], pseudo_hbm.at[pl.ds(t * TILE, TILE)], sem_out.at[t]
        )
        cp.start()
        copies_out.append(cp)
    cert = 1.0 - (jnp.log(total) - moment / total) / jnp.log(jnp.float32(CLS))
    for t in range(TPD):
        cert_ref[2 * t : 2 * t + 1, :] = cert[t : t + 1, :HALF]
        cert_ref[2 * t + 1 : 2 * t + 2, :] = cert[t : t + 1, HALF:]
    for cp in copies_out:
        cp.wait()


def local(prior, blocks, links, counts, fetch, seeds, inv_temp):
    bf, f32 = jnp.bfloat16, jnp.float32
    vmem = pltpu.VMEM
    expo, stats = pl.pallas_call(
        kernel,
        out_shape=(
            jax.ShapeDtypeStruct((TPD, TILE, TILE), bf),
            jax.ShapeDtypeStruct((4, 3, TPD, TILE), f32),
        ),
        in_specs=[pl.BlockSpec(memory_space=pl.ANY)] * 7,
        out_specs=(pl.BlockSpec(memory_space=pl.ANY), pl.BlockSpec(memory_space=pl.ANY)),
        scratch_shapes=[
            vmem((TPD * TILE, W), bf),
            vmem((TPD, NB, TILE, TILE), bf),
            vmem((TPD, TILE, TILE), f32),
            vmem((TILE, TILE), f32),
            vmem((TPD, TILE, TILE), bf),
            vmem((TPD, TILE, TILE), bf),
            vmem((4, 7, 4, Q, TILE), bf),
            vmem((16, 8, 128), jnp.int32),
            pltpu.SMEM((16, 8, 128), jnp.int32),
            pltpu.SMEM((TPD * NB,), jnp.int32),
            pltpu.SMEM((TPD * NB,), jnp.int32),
            vmem((TPD, TILE, 1), jnp.int32),
            vmem((TPD, TILE), f32),
            vmem((TPD, TILE, TILE), bf),
            vmem((4, 3, TPD, TILE), f32),
            vmem((TPD, TILE), jnp.int32),
        ]
        + [vmem((3, TPD, Q, TILE), bf) for _ in range(8)]
        + [vmem((2, 4, Q, TILE), bf) for _ in range(8)]
        + [vmem((ZERO + 1, Q, TILE), bf) for _ in range(8)]
        + [
            pltpu.SemaphoreType.DMA((4, NAMES)),
            pltpu.SemaphoreType.DMA((8, NAMES)),
            pltpu.SemaphoreType.DMA((14,)),
            pltpu.SemaphoreType.DMA((14,)),
            pltpu.SemaphoreType.DMA((3,)),
            pltpu.SemaphoreType.DMA((3,)),
            pltpu.SemaphoreType.DMA((TPD,)),
            pltpu.SemaphoreType.DMA((10,)),
            pltpu.SMEM((TPD, NB), jnp.int32),
            pltpu.SMEM((TPD,), jnp.int32),
            vmem((1, 32), jnp.int32),
            vmem((16, 128), jnp.int32),
            vmem((16, 128), f32),
            pltpu.SemaphoreType.DMA((5,)),
        ],
        compiler_params=pltpu.CompilerParams(
            collective_id=0, has_side_effects=True, vmem_limit_bytes=VLIM
        ),
        name="propagate",
    )(
        links, counts, fetch.reshape(1, -1), prior, blocks,
        seeds.reshape(16, 128), inv_temp.reshape(16, 128),
    )
    pseudo, cert = pl.pallas_call(
        finish,
        out_shape=(
            jax.ShapeDtypeStruct((TPD * TILE, W), bf),
            jax.ShapeDtypeStruct((16, 128), f32),
        ),
        in_specs=[
            pl.BlockSpec(memory_space=pl.ANY),
            pl.BlockSpec(memory_space=pl.ANY),
        ],
        out_specs=(pl.BlockSpec(memory_space=pl.ANY), pl.BlockSpec(memory_space=pltpu.VMEM)),
        scratch_shapes=[
            vmem((TPD, TILE, TILE), bf),
            vmem((TPD * TILE, W), bf),
            vmem((4, 3, TPD, TILE), f32),
            pltpu.SemaphoreType.DMA((TPD + 1,)),
            pltpu.SemaphoreType.DMA((TPD,)),
        ],
        name="finish",
    )(expo, stats)
    return pseudo, cert.reshape(-1)


def solution(mesh):
    return jax.shard_map(
        local,
        mesh=mesh,
        in_specs=(
            P("rows", "cls"),
            P("rows", None, None, None),
            P("rows", None),
            P("rows"),
            P("rows", None, None),
            P("rows"),
            P("rows"),
        ),
        out_specs=(P("rows", "cls"), P("rows")),
        check_vma=False,
    )
```

```python
import functools
import math

import jax
import jax.numpy as jnp
from jax import lax
from jax.experimental import pallas as pl
from jax.experimental.pallas import tpu as pltpu
from jax.sharding import PartitionSpec as P

CLS = 1000
NB = 24
TPD = 8
TILE = 256
W = 250
HALF = 128
Q = 64
VLIM = 66_000_000
ZERO = 40

BLEND = 0.8
MESH = pl.DeviceIdType.MESH

GR, GL, FR, FL = (0, 1, 2, 3), (4, 5, 6, 7), (8, 9), (10, 11)
RR, RL, D0R, D1R, D0L, D1L, WR, WL, PT = range(12, 21)
NAMES = 21

PEERS = [(0, dz, dc) for dz in range(4) for dc in range(2) if (dz, dc) != (0, 0)] + [
    (dx, 0, dc) for dx in range(1, 4) for dc in range(2)
]


def kernel(
    links_hbm, counts_hbm, fetch_hbm, prior_hbm, blocks_hbm, seeds_hbm, temp_hbm,
    expo_hbm, stats_out,
    *scratch,
):
    (pv, bv, acc, raw, fld0, fld1, stage, frv, frm, tab_a, tab_b, seed_c, temp_r) = scratch[:13]
    expos, stats, seed_r = scratch[13:16]
    links_ref, counts_ref, fetch_ref, seeds_ref, temp_ref, small = scratch[-6:]
    gb = scratch[16:24]
    rl = scratch[24:32]
    cs = scratch[32:40]
    (send, recv, f_send, f_recv, y_send, y_recv, b_sem, loc) = scratch[40:-6]
    fld = (fld0, fld1)

    r = lax.axis_index("rows")
    y = lax.axis_index("cls")
    c = lax.rem(r, 2)
    x = lax.rem(r // 2, 4)
    z = r // 8

    def dev(dx, dz, dc):
        row = (lax.rem(z + dz, 4) * 4 + lax.rem(x + dx, 4)) * 2 + lax.rem(c + dc, 2)
        return (y, row)

    def idx(rnd, rt, kh):
        return (rnd * 2 + rt) * 2 + kh

    def step(rt, d, dc):
        return dev(0, d % 4, dc) if rt == 0 else dev(d % 4, 0, dc)

    def gstep(rt, d):
        return dev(d % 4, 0, 0) if rt == 0 else dev(0, d % 4, 0)

    block_cps = [
        pltpu.make_async_copy(blocks_hbm.at[t], bv.at[t], b_sem.at[t]) for t in range(TPD)
    ]
    barrier = pltpu.get_barrier_semaphore()
    for p in PEERS:
        pl.semaphore_signal(barrier, inc=1, device_id=dev(*p), device_id_type=MESH)
    for dy in range(1, 4):
        pl.semaphore_signal(
            barrier, inc=1, device_id=(lax.rem(y + dy, 4), r), device_id_type=MESH
        )
    prior_cp = pltpu.make_async_copy(prior_hbm, pv, loc.at[0])
    prior_cp.start()
    small_cps = [
        pltpu.make_async_copy(src, dst, small.at[k])
        for k, (src, dst) in enumerate(
            [
                (fetch_hbm, fetch_ref), (links_hbm, links_ref), (counts_hbm, counts_ref),
                (seeds_hbm, seeds_ref), (temp_hbm, temp_ref),
            ]
        )
    ]
    for cp in small_cps:
        cp.start()
    small_cps[0].wait()
    frv[0] = jnp.zeros((8, 128), jnp.int32)
    frv[0, 0:1, 0:32] = fetch_ref[...]
    frv[8] = jnp.zeros((8, 128), jnp.int32)
    frv[8, 0:1, 0:32] = fetch_ref[...]
    prior_cp.wait()
    for t in range(TPD):
        fld0[t, :, HALF:] = jnp.zeros((TILE, HALF), jnp.bfloat16)
        fld0[t, :, :W] = pv[t * TILE : (t + 1) * TILE, :]
    pl.semaphore_wait(barrier, len(PEERS) + 3)

    def g_copy(rnd, rt, kh, name):
        i = idx(rnd, rt, kh)
        rows = pl.ds(kh * HALF + rt * Q, Q)
        if name in GR or name in GL:
            pair = pl.ds(2 * (name % 4), 2)
            d, far = (1, 2) if name in GR else (-1, 0)
            src, dst = fld[rnd].at[pair, rows, :], gb[i].at[far, pair]
        else:
            d, far = (1, 2) if name in FR else (-1, 0)
            pair = pl.ds(2 * (name - 8), 2)
            src, dst = gb[i].at[far, pair], gb[i].at[1, pair]
        return pltpu.make_async_remote_copy(
            src_ref=src, dst_ref=dst, send_sem=send.at[idx(0, rt, kh), name],
            recv_sem=recv.at[i, name], device_id=gstep(rt, d), device_id_type=MESH,
        )

    def p_copy(rnd, rt, kh, name):
        i = idx(rnd, rt, kh)
        s = idx(0, rt, kh)
        group = lambda g: stage.at[s, g]
        slot = lambda d, dc: cs[i].at[pl.ds((d * 2 + dc) * 4, 4)]
        src, dst, d, dc = {
            RR: (group(2), rl[i].at[0], 1, 0),
            RL: (group(3), rl[i].at[1], -1, 0),
            D0R: (group(0), slot(3, 0), 1, 0),
            D1R: (group(1), slot(3, 1), 1, 1),
            D0L: (group(4), slot(1, 0), -1, 0),
            D1L: (group(5), slot(1, 1), -1, 1),
            WR: (rl[i].at[0], slot(2, 0), 1, 0),
            WL: (rl[i].at[1], slot(2, 1), -1, 1),
            PT: (group(6), slot(0, 1), 0, 1),
        }[name]
        return pltpu.make_async_remote_copy(
            src_ref=src, dst_ref=dst, send_sem=send.at[s, name],
            recv_sem=recv.at[i, name], device_id=step(rt, d, dc), device_id_type=MESH,
        )

    def start_g(rnd, kh, names):
        for name in names:
            for rt in range(2):
                g_copy(rnd, rt, kh, name).start()

    def wait_g(rnd, kh, names):
        for name in names:
            for rt in range(2):
                g_copy(rnd, rt, kh, name).wait_recv()

    def start_p(rnd, kh, names):
        for name in names:
            for rt in range(2):
                p_copy(rnd, rt, kh, name).start()

    def wait_p(rnd, kh, names):
        for name in names:
            for rt in range(2):
                p_copy(rnd, rt, kh, name).wait_recv()

    def wait_sends(kh, rnd):
        for rt in range(2):
            for name in GR + GL + FR + FL:
                g_copy(rnd, rt, kh, name).wait_send()
            for name in (RR, RL, D0R, D1R, D0L, D1L, WR, WL, PT):
                p_copy(rnd, rt, kh, name).wait_send()

    f_copies = []
    for k, (dx, dz, dc, base) in enumerate(
        [(0, dz, dc, 0) for dz in range(4) for dc in range(2) if (dz, dc) != (0, 0)]
        + [(dx, 0, dc, 8) for dx in range(4) for dc in range(2) if (dx, dc) != (0, 0)]
    ):
        d = dz if base == 0 else dx
        f_copies.append(
            pltpu.make_async_remote_copy(
                src_ref=frv.at[0], dst_ref=frv.at[base + ((4 - d) % 4) * 2 + dc],
                send_sem=f_send.at[k], recv_sem=f_recv.at[k],
                device_id=dev(dx, dz, dc), device_id_type=MESH,
            )
        )

    def src_row(rt, d):
        if rt == 0:
            return (z * 4 + lax.rem(x + d, 4)) * 2 + c
        return (lax.rem(z + d, 4) * 4 + x) * 2 + c

    def select(rnd, kh):
        for rt in range(2):
            i = idx(rnd, rt, kh)
            rows = pl.ds(kh * HALF + rt * Q, Q)
            for d in range(4):
                row = src_row(rt, d)
                for dd in (2, 1, 3, 0):
                    for dc in range(2):
                        f = frm[rt * 8 + dd * 2 + dc, 0, row]
                        value = fld[rnd][f, rows, :] if d == 0 else gb[i][d - 1, f]
                        if (dd, dc) == (0, 0):
                            cs[i][d] = value
                        else:
                            g = 6 if dd == 0 else (dd - 1) * 2 + dc
                            stage[idx(0, rt, kh), g, d] = value

    def own_slots(rnd, t):
        for rt in range(2):
            for kh in range(2):
                a = kh * HALF + rt * Q
                cs[idx(rnd, rt, kh)][4 * TPD + t] = fld[rnd][t, a : a + Q, :]

    def product(rnd, kh, t):
        a = idx(rnd, 0, kh)
        b = idx(rnd, 1, kh)
        total = None
        for jp in range(NB // 2):
            left, right = [], []
            for j in (2 * jp, 2 * jp + 1):
                left.append(bv[t, j, :, kh * HALF : (kh + 1) * HALF])
                right.append(cs[a][tab_a[t * NB + j]])
                right.append(cs[b][tab_b[t * NB + j]])
            d = jnp.dot(
                jnp.concatenate(left, axis=1), jnp.concatenate(right, axis=0),
                preferred_element_type=jnp.float32,
            )
            total = d if total is None else total + d
        return total

    lane = lax.broadcasted_iota(jnp.int32, (TILE, TILE), 1)
    inside = lane < W
    column = lane + y * W

    def mixed(t, total):
        hit = (seed_c[t] == column) & inside
        return BLEND * total + jnp.where(hit, jnp.float32(1.0 - BLEND), jnp.float32(0.0))

    HOP = ((GR[0], GL[0]), (GR[2], GL[2]), (GR[1], GL[1]), (GR[3], GL[3]))
    ALL_HOPS = sum(HOP, ())
    GO_ON = (((GR[0], FR[0]), (GL[2], FL[0])), ((GR[1], FR[1]), (GL[3], FL[1])))
    REST = (GR[2], GR[3], GL[0], GL[1]) + FR + FL
    SENDS = (RR, RL, D0R, D0L, D1R, D1L, PT)
    RELAY = (WR, WL)
    FINAL = (D0R, D0L, D1R, D1L, PT, WR, WL)

    for cp in f_copies:
        cp.start()
    start_g(0, 0, ALL_HOPS)
    for cp in block_cps:
        cp.start()

    for rnd in range(2):
        for rt in range(2):
            for kh in range(2):
                cs[idx(rnd, rt, kh)][ZERO] = jnp.zeros((Q, TILE), jnp.bfloat16)
    for t in range(TPD):
        own_slots(0, t)

    def forward(rnd, kh):
        for part in GO_ON:
            for name, onward in part:
                wait_g(rnd, kh, (name,))
                start_g(rnd, kh, (onward,))

    def prepare():
        for cp in small_cps[1:]:
            cp.wait()
        seeds_t = jnp.transpose(seeds_ref[...].astype(jnp.float32), (1, 0))
        for t in range(TPD):
            for h in range(2):
                k = 2 * t + h
                seed_c[t, h * HALF : (h + 1) * HALF, :] = seeds_t[:, k : k + 1].astype(jnp.int32)
                half = slice(h * HALF, (h + 1) * HALF)
                seed_r[t : t + 1, half] = seeds_ref[k : k + 1, :]
                temp_r[t : t + 1, half] = temp_ref[k : k + 1, :]
        for cp in f_copies:
            cp.wait()
        to_smem = pltpu.make_async_copy(frv, frm, loc.at[1])
        to_smem.start()

        def slots(t, carry):
            count = counts_ref[t]
            for j in range(NB):
                v = links_ref[t, j]
                s = jnp.maximum(v - TPD, 0)
                dz = ((s >> 3) + 4 - z) & 3
                dx = (((s >> 1) & 3) + 4 - x) & 3
                dc = (s + c) & 1
                own = v < TPD
                live = j < count
                sa = jnp.where(own, 4 * TPD + v, (dz * 2 + dc) * 4 + dx)
                sb = jnp.where(own, 4 * TPD + v, (dx * 2 + dc) * 4 + dz)
                tab_a[t * NB + j] = jnp.where(live, sa, ZERO)
                tab_b[t * NB + j] = jnp.where(live, sb, ZERO)
            return carry

        lax.fori_loop(0, TPD, slots, 0)
        to_smem.wait()

    def exchange(rnd):
        forward(rnd, 0)
        start_g(rnd, 1, ALL_HOPS)
        if rnd == 0:
            prepare()
        wait_g(rnd, 0, REST)
        select(rnd, 0)
        start_p(rnd, 0, SENDS)
        forward(rnd, 1)
        wait_g(rnd, 1, REST)
        select(rnd, 1)
        wait_p(rnd, 0, (RR, RL))
        start_p(rnd, 0, RELAY)
        start_p(rnd, 1, SENDS)
        wait_p(rnd, 0, FINAL)

    def first_chunk(rnd):
        def body(t, carry):
            @pl.when(t == 4)
            def _():
                wait_p(rnd, 1, (RR, RL))
                start_p(rnd, 1, RELAY)

            acc[t] = product(rnd, 0, t)
            return carry

        lax.fori_loop(0, TPD, body, 0)
        wait_p(rnd, 1, FINAL)

    exchange(0)
    for cp in block_cps:
        cp.wait()
    first_chunk(0)
    for kh in range(2):
        wait_sends(kh, 0)

    def first_tile(i, carry):
        for k in range(3):

            @pl.when(i == 2 * k + 2)
            def _():
                start_g(1, 0, HOP[k])

        t = (i // 4) * 2 + ((i // 2) % 2) * 4 + i % 2
        value = mixed(t, acc[t] + product(0, 1, t)).astype(jnp.bfloat16)
        fld1[t] = value
        for rt in range(2):
            for kh in range(2):
                a = kh * HALF + rt * Q
                cs[idx(1, rt, kh)][4 * TPD + t] = value[a : a + Q, :]
        return carry

    lax.fori_loop(0, TPD, first_tile, 0)
    start_g(1, 0, HOP[3])

    exchange(1)
    first_chunk(1)

    class_no = lax.broadcasted_iota(jnp.int32, (TILE, TILE), 0)
    real = class_no < W
    class_no = class_no + y * W

    def softmax(t):
        total = jnp.transpose(raw[...], (1, 0))
        hit = (seed_r[pl.ds(t, 1), :] == class_no) & real
        total = BLEND * total + jnp.where(hit, jnp.float32(1.0 - BLEND), jnp.float32(0.0))
        logits = temp_r[pl.ds(t, 1), :] * total
        top = jnp.max(jnp.where(real, logits, -jnp.inf), axis=0, keepdims=True)
        shifted = jnp.where(real, logits - top, 0.0)
        expo = jnp.where(real, jnp.exp(shifted), 0.0)
        return expo, (
            top,
            jnp.sum(expo, axis=0, keepdims=True),
            jnp.sum(expo * shifted, axis=0, keepdims=True),
        )

    def keep(t, expo, stat):
        expos[t] = jnp.transpose(expo, (1, 0)).astype(jnp.bfloat16)
        for k in range(3):
            stats[y, k, pl.ds(t, 1), :] = stat[k]

    def y_copy(dy, slot):
        return pltpu.make_async_remote_copy(
            src_ref=stats.at[y], dst_ref=stats.at[slot],
            send_sem=y_send.at[dy - 1], recv_sem=y_recv.at[dy - 1],
            device_id=(lax.rem(y + dy, 4), r), device_id_type=MESH,
        )

    def out_copy(t):
        return pltpu.make_async_copy(expos.at[t], expo_hbm.at[t], loc.at[2 + t])

    def last_tile(t, carry):
        before = jnp.maximum(t - 1, 0)
        expo, stat = softmax(before)
        total = acc[t] + product(1, 1, t)
        keep(before, expo, stat)
        raw[...] = total

        @pl.when(t == 5)
        def _():
            for k in range(4):
                out_copy(k).start()

        return carry

    raw[...] = jnp.zeros((TILE, TILE), jnp.float32)
    lax.fori_loop(0, TPD, last_tile, 0)
    keep(TPD - 1, *softmax(TPD - 1))
    for dy in (2, 1, 3):
        y_copy(dy, y).start()
    for k in range(4, TPD):
        out_copy(k).start()
    for kh in range(2):
        wait_sends(kh, 1)
    for k in range(TPD):
        out_copy(k).wait()
    for dy in range(1, 4):
        y_copy(dy, y).wait_send()
        y_copy(dy, lax.rem(y + 4 - dy, 4)).wait_recv()
    stats_cp = pltpu.make_async_copy(stats, stats_out, loc.at[1])
    stats_cp.start()
    stats_cp.wait()


def finish(expo_hbm, stats_hbm, pseudo_hbm, cert_ref, ev, outv, stats, sem_in, sem_out):
    y = lax.axis_index("cls")
    stats_cp = pltpu.make_async_copy(stats_hbm, stats, sem_in.at[TPD])
    stats_cp.start()
    copies_in, copies_out = [], []
    for t in range(TPD):
        cp = pltpu.make_async_copy(expo_hbm.at[t], ev.at[t], sem_in.at[t])
        cp.start()
        copies_in.append(cp)
    stats_cp.wait()
    top = functools.reduce(jnp.maximum, [stats[k, 0] for k in range(4)])
    total = jnp.zeros((TPD, TILE), jnp.float32)
    moment = jnp.zeros((TPD, TILE), jnp.float32)
    for k in range(4):
        diff = stats[k, 0] - top
        scale = jnp.exp(diff)
        total = total + scale * stats[k, 1]
        moment = moment + scale * (stats[k, 2] + stats[k, 1] * diff)
    factor = jnp.transpose(jnp.exp(stats[y, 0] - top) / total, (1, 0))
    for t in range(TPD):
        copies_in[t].wait()
        rows = slice(t * TILE, (t + 1) * TILE)
        part = ev[t].astype(jnp.float32) * factor[:, t : t + 1]
        outv[rows, :] = part.astype(jnp.bfloat16)[:, :W]
        cp = pltpu.make_async_copy(
            outv.at[pl.ds(t * TILE, TILE)], pseudo_hbm.at[pl.ds(t * TILE, TILE)], sem_out.at[t]
        )
        cp.start()
        copies_out.append(cp)
    cert = 1.0 - (jnp.log(total) - moment / total) / jnp.log(jnp.float32(CLS))
    for t in range(TPD):
        cert_ref[2 * t : 2 * t + 1, :] = cert[t : t + 1, :HALF]
        cert_ref[2 * t + 1 : 2 * t + 2, :] = cert[t : t + 1, HALF:]
    for cp in copies_out:
        cp.wait()


def local(prior, blocks, links, counts, fetch, seeds, inv_temp):
    bf, f32 = jnp.bfloat16, jnp.float32
    vmem = pltpu.VMEM
    expo, stats = pl.pallas_call(
        kernel,
        out_shape=(
            jax.ShapeDtypeStruct((TPD, TILE, TILE), bf),
            jax.ShapeDtypeStruct((4, 3, TPD, TILE), f32),
        ),
        in_specs=[pl.BlockSpec(memory_space=pl.ANY)] * 7,
        out_specs=(pl.BlockSpec(memory_space=pl.ANY), pl.BlockSpec(memory_space=pl.ANY)),
        scratch_shapes=[
            vmem((TPD * TILE, W), bf),
            vmem((TPD, NB, TILE, TILE), bf),
            vmem((TPD, TILE, TILE), f32),
            vmem((TILE, TILE), f32),
            vmem((TPD, TILE, TILE), bf),
            vmem((TPD, TILE, TILE), bf),
            vmem((4, 7, 4, Q, TILE), bf),
            vmem((16, 8, 128), jnp.int32),
            pltpu.SMEM((16, 8, 128), jnp.int32),
            pltpu.SMEM((TPD * NB,), jnp.int32),
            pltpu.SMEM((TPD * NB,), jnp.int32),
            vmem((TPD, TILE, 1), jnp.int32),
            vmem((TPD, TILE), f32),
            vmem((TPD, TILE, TILE), bf),
            vmem((4, 3, TPD, TILE), f32),
            vmem((TPD, TILE), jnp.int32),
        ]
        + [vmem((3, TPD, Q, TILE), bf) for _ in range(8)]
        + [vmem((2, 4, Q, TILE), bf) for _ in range(8)]
        + [vmem((ZERO + 1, Q, TILE), bf) for _ in range(8)]
        + [
            pltpu.SemaphoreType.DMA((4, NAMES)),
            pltpu.SemaphoreType.DMA((8, NAMES)),
            pltpu.SemaphoreType.DMA((14,)),
            pltpu.SemaphoreType.DMA((14,)),
            pltpu.SemaphoreType.DMA((3,)),
            pltpu.SemaphoreType.DMA((3,)),
            pltpu.SemaphoreType.DMA((TPD,)),
            pltpu.SemaphoreType.DMA((10,)),
            pltpu.SMEM((TPD, NB), jnp.int32),
            pltpu.SMEM((TPD,), jnp.int32),
            vmem((1, 32), jnp.int32),
            vmem((16, 128), jnp.int32),
            vmem((16, 128), f32),
            pltpu.SemaphoreType.DMA((5,)),
        ],
        compiler_params=pltpu.CompilerParams(
            collective_id=0, has_side_effects=True, vmem_limit_bytes=VLIM
        ),
        name="propagate",
    )(
        links, counts, fetch.reshape(1, -1), prior, blocks,
        seeds.reshape(16, 128), inv_temp.reshape(16, 128),
    )
    pseudo, cert = pl.pallas_call(
        finish,
        out_shape=(
            jax.ShapeDtypeStruct((TPD * TILE, W), bf),
            jax.ShapeDtypeStruct((16, 128), f32),
        ),
        in_specs=[
            pl.BlockSpec(memory_space=pl.ANY),
            pl.BlockSpec(memory_space=pl.ANY),
        ],
        out_specs=(pl.BlockSpec(memory_space=pl.ANY), pl.BlockSpec(memory_space=pltpu.VMEM)),
        scratch_shapes=[
            vmem((TPD, TILE, TILE), bf),
            vmem((TPD * TILE, W), bf),
            vmem((4, 3, TPD, TILE), f32),
            pltpu.SemaphoreType.DMA((TPD + 1,)),
            pltpu.SemaphoreType.DMA((TPD,)),
        ],
        name="finish",
    )(expo, stats)
    return pseudo, cert.reshape(-1)


def solution(mesh):
    return jax.shard_map(
        local,
        mesh=mesh,
        in_specs=(
            P("rows", "cls"),
            P("rows", None, None, None),
            P("rows", None),
            P("rows"),
            P("rows", None, None),
            P("rows"),
            P("rows"),
        ),
        out_specs=(P("rows", "cls"), P("rows")),
        check_vma=False,
    )
```
